32 devices in a mesh: seq: 16 (over z, y, core), head: 2 (over x).
Axes of the slice: x: 2, y: 2, z: 4, core: 2. Of those that a mesh axis runs over, the one named last changes fastest.
Arguments:
- qkv: bfloat16 [3, 2048, 1024], P(None, ('seq', 'head')), may hold values from -128 to 128
- token_rate: float32 [2048, 2], P('seq', 'head'), may hold values from 0.1 to 1
- head_rate: float32 [2], P('head'), may hold values from 0.5 to 2
- fast_state: float32 [3, 2, 512, 512], P(None, 'head', 'seq'), may hold values from -0.25 to 0.25
Outputs:
- combined: bfloat16 [2048, 1024], P(('seq', 'head'))
- new_state: float32 [3, 2, 512, 512], P(None, 'head', 'seq')
The draws below stay inside these ranges and needn't reach their ends.
All inputs are finite; a program needn't handle non-finite values.
Results may differ from the reference program's by a relative error of at most 0.017.
Values may be sent and summed in bfloat16 or wider, within the bound.
A program may use at most 64 MiB of HBM per device.

```python
import math
import jax
import jax.numpy as jnp
from jax import lax

HD = 512
FH = 512
HEADS = 2
TOK_DEV = 128
TOKENS = 2048
WINDOW = 1024
NS_STEPS = 2


def draw_qkv(key, part):
    feature_count = HEADS * HD
    branches = jax.random.split(key, 1)
    drawn = jnp.clip(jax.random.normal(branches[0], (3, TOKENS, feature_count), jnp.float32), -6.0, 6.0)
    drawn = drawn * jnp.array([1.0, 1.0, 2.0], jnp.float32)[:, None, None]
    return drawn.astype(jnp.bfloat16)


def steps_of(key, shape, cuts, smallest, high):
    level = 1.0
    for position, blocks in cuts:
        steps = jax.random.uniform(jax.random.fold_in(jax.random.fold_in(key, 6), position), (blocks,), jnp.float32, smallest / len(cuts), high / len(cuts))
        level = level * jnp.repeat(jnp.exp(steps), shape[position] // blocks).reshape((-1,) + (1,) * (len(shape) - 1 - position))
    return level


def bell_draw(rng, shape, width, limit, cuts=(), kind=jnp.bfloat16):
    loudness = steps_of(rng, shape, cuts, -0.22, 0.18) if cuts else 1.0
    values = jax.random.normal(rng, shape, jnp.float32) * width * loudness
    return jnp.minimum(jnp.maximum(values, -limit), limit).astype(kind)


def setup_inputs(seed: int = 0) -> dict:
    streams_of = jax.random.split(jax.random.key(seed), 5)
    qkv = draw_qkv(jax.random.fold_in(streams_of[4], 71), 0)
    token_rate = jnp.clip(jnp.exp(math.log(1.0) - 2.3025851 * jax.random.uniform(streams_of[1], (TOKENS, HEADS), jnp.float32) ** steps_of(streams_of[1], (TOKENS, HEADS), ((0, 16), (1, 2)), -0.2, 0.2)), 0.1, 1.0)
    head_rate = jnp.clip(jnp.exp(math.log(2.0) - 1.3862944 * jax.random.uniform(streams_of[2], (HEADS,), jnp.float32) ** steps_of(streams_of[2], (HEADS,), ((0, 2),), -0.2, 0.2)), 0.5, 2.0)
    fast_state = bell_draw(streams_of[3], (3, HEADS, FH, HD), HD ** -0.5, 0.25, ((1, 2), (2, 16)), jnp.float32)
    return {"qkv": qkv, "token_rate": token_rate, "head_rate": head_rate, "fast_state": fast_state}


ns_first = 3.4445
ns_second = -4.775
ns_third = 2.0315
rms_eps = 1e-06
norm_eps = 1e-07
precise = lax.Precision.HIGHEST

def rms_scaled(values):
    return values * lax.rsqrt(lax.optimization_barrier(jnp.mean(values * values, axis=-1, keepdims=True)) + rms_eps)

def contract_last(left_side, right_side):
    return lax.dot_general(left_side, right_side, (((1,), (1,)), ((), ())), preferred_element_type=jnp.float32)

def contract_first(left_side, right_side):
    return lax.dot_general(left_side, right_side, (((0,), (0,)), ((), ())), preferred_element_type=jnp.float32)

def head_gradient(key_norm, signal, weight_piece):
    gate_act = contract_last(key_norm, weight_piece[0])
    up_act = contract_last(key_norm, weight_piece[1])
    active = (jax.nn.silu(gate_act) * up_act).astype(jnp.bfloat16)
    back_grad = contract_last(signal, weight_piece[2])
    sigmoid_gate = jax.nn.sigmoid(gate_act)
    grad_gate = (back_grad * up_act * sigmoid_gate * (1.0 + gate_act * (1.0 - sigmoid_gate))).astype(jnp.bfloat16)
    grad_up = (back_grad * jax.nn.silu(gate_act)).astype(jnp.bfloat16)
    return jnp.stack([contract_first(grad_gate, key_norm), contract_first(grad_up, key_norm), contract_first(active, signal)])

def window_attention(queries, keys_head, values_head):
    pad_rows = jnp.zeros((WINDOW, HD), jnp.bfloat16)
    padded_keys = jnp.concatenate([pad_rows, keys_head], axis=0)
    padded_values = jnp.concatenate([pad_rows, values_head], axis=0)
    starts = jnp.arange(TOKENS // TOK_DEV, dtype=jnp.int32) * TOK_DEV

    def one_block(block_start):
        query_block = lax.dynamic_slice_in_dim(queries, block_start, TOK_DEV, 0)
        key_block = lax.dynamic_slice_in_dim(padded_keys, block_start, WINDOW + TOK_DEV, 0)
        value_block = lax.dynamic_slice_in_dim(padded_values, block_start, WINDOW + TOK_DEV, 0)
        scores = contract_last(query_block, key_block) * HD ** (-0.5)
        query_pos = block_start + jnp.arange(TOK_DEV, dtype=jnp.int32)[:, None]
        key_pos = block_start - WINDOW + jnp.arange(WINDOW + TOK_DEV, dtype=jnp.int32)[None, :]
        visible = (key_pos <= query_pos) & (key_pos > query_pos - WINDOW) & (key_pos >= 0)
        scores = jnp.where(visible, scores, -jnp.inf)
        row_max = lax.optimization_barrier(jnp.max(scores, axis=1, keepdims=True))
        exp_scores = jnp.exp(scores - row_max)
        weights = (exp_scores / lax.optimization_barrier(jnp.sum(exp_scores, axis=1, keepdims=True))).astype(jnp.bfloat16)
        return jnp.dot(weights, value_block, preferred_element_type=jnp.float32)
    return lax.map(one_block, starts).reshape(TOKENS, HD)

def newton_schulz(gradients):
    frob_norm = jnp.sqrt(lax.optimization_barrier(jnp.sum(gradients * gradients, axis=(1, 2), keepdims=True)))
    iterate = gradients / (frob_norm + norm_eps)
    for section_number in range(NS_STEPS):
        gram_matrix = jnp.einsum('mij,mkj->mik', iterate, iterate, precision=precise)
        poly_part = ns_second * gram_matrix + ns_third * jnp.einsum('mij,mjk->mik', gram_matrix, gram_matrix, precision=precise)
        iterate = ns_first * iterate + jnp.einsum('mij,mjk->mik', poly_part, iterate, precision=precise)
    return iterate

def one_head(packed):
    queries, keys_head, values_head, token_rates, step_size, head_state = packed
    query_norm = rms_scaled(queries.astype(jnp.float32)).astype(jnp.bfloat16)
    key_norm = rms_scaled(keys_head.astype(jnp.float32)).astype(jnp.bfloat16)
    signal = (-token_rates[:, None] * values_head.astype(jnp.float32)).astype(jnp.bfloat16)
    gradients = head_gradient(key_norm, signal, head_state.astype(jnp.bfloat16))
    updated = head_state - step_size * newton_schulz(gradients)
    new_low = updated.astype(jnp.bfloat16)
    gate_act = contract_last(query_norm, new_low[0])
    up_act = contract_last(query_norm, new_low[1])
    active = (jax.nn.silu(gate_act) * up_act).astype(jnp.bfloat16)
    fast_out = jnp.dot(active, new_low[2], preferred_element_type=jnp.float32)
    attention = window_attention(queries, keys_head, values_head)
    return ((attention + fast_out).astype(jnp.bfloat16), updated)

def reference(qkv, token_rate, head_rate, fast_state):
    split_heads = qkv.reshape(3, TOKENS, HEADS, HD).transpose(0, 2, 1, 3)
    outputs, states = lax.map(one_head, (split_heads[0], split_heads[1], split_heads[2], token_rate.T, head_rate, fast_state.transpose(1, 0, 2, 3)))
    combined = outputs.transpose(1, 0, 2).reshape(TOKENS, HEADS * HD)
    return (combined, states.transpose(1, 0, 2, 3))
```

```python
import functools

import jax
import jax.numpy as jnp
from jax import lax
from jax.experimental import pallas as pl
from jax.experimental.pallas import tpu as pltpu
from jax.sharding import PartitionSpec as P

WINDOW = 1024
NS_STEPS = 2

ns_first = 3.4445
ns_second = -4.775
ns_third = 2.0315
rms_eps = 1e-06
norm_eps = 1e-07

MESH = pl.DeviceIdType.MESH
CORES = 2
MATS = 3


def rms_scaled(values):
    return values * lax.rsqrt(jnp.mean(values * values, axis=-1, keepdims=True) + rms_eps)


def contract_last(left_side, right_side):
    return lax.dot_general(
        left_side, right_side, (((1,), (1,)), ((), ())), preferred_element_type=jnp.float32
    )


def low(values):
    return values.astype(jnp.bfloat16)


def dot(left_side, right_side):
    return jnp.dot(left_side, right_side, preferred_element_type=jnp.float32)


def kernel(
    sizes,
    qkv, rate, head_rate, state,
    out, new,
    kv, q, w, gfull, gsend, grecv, g, wnew, direction, rates, comb,
    att_max, att_sum, att_acc, gate_q,
    local_sem, x_sem, q_sem, rate_sem, ky_sem, ks_sem, wz_sem, wy_sem, ws_sem,
    rs_sem, gz_sem, gy_sem, gs_sem, cz_sem, cy_sem, cs_sem, o_sem,
):
    heads, planes, plane, back = sizes
    rows_y = plane // CORES
    part = qkv.shape[1]
    tokens, width = q.shape
    hidden = direction.shape[0]
    state_rows = state.shape[1]
    link = w.dtype

    seq = lax.axis_index("seq")
    head = lax.axis_index("head")
    z = seq // plane
    p = lax.rem(seq, plane)
    y = p // CORES
    core = lax.rem(p, CORES)

    def device(z_at, p_at):
        return {"seq": z_at * plane + p_at, "head": head}

    def z_up(step):
        return lax.rem(z + step, planes)

    def p_of_y(step):
        return lax.rem(y + step, rows_y) * CORES + core

    sibling = y * CORES + (1 - core)

    def head_peer(step):
        return {"seq": seq, "head": lax.rem(head + step, heads)}

    peers = [head_peer(step) for step in range(1, heads)]
    peers += [device(z, lax.rem(p + step, plane)) for step in range(1, plane)]
    peers += [device(z_up(step), p) for step in range(1, planes)]
    barrier = pltpu.get_barrier_semaphore()
    for peer in peers:
        pl.semaphore_signal(barrier, inc=1, device_id=peer, device_id_type=MESH)

    started = []

    def send(src, dst, sem, place, target, when=None):
        copy = pltpu.make_async_remote_copy(
            src_ref=src,
            dst_ref=dst,
            send_sem=sem.at[(0,) + place],
            recv_sem=sem.at[(1,) + place],
            device_id=target,
            device_id_type=MESH,
        )
        if when is None:
            copy.start()
        else:
            pl.when(when)(copy.start)
        started.append((copy, when))
        return copy

    def part_rows(step):
        owner = lax.rem(head - step + heads, heads)
        return pl.ds(pl.multiple_of(owner * part, part), part)

    def head_columns(index):
        return pl.ds(pl.multiple_of(index * width, width), width)

    own_rows = part_rows(0)
    own_columns = head_columns(head)
    rates[p] = rate[...]
    for mat in range(MATS):
        w[mat, z, p] = state[mat].astype(link)
    pl.semaphore_wait(barrier, len(peers))

    x_copies = [
        send(
            qkv.at[pl.ds(1, 2), :, head_columns(lax.rem(head + step, heads))],
            kv.at[0, :, p, own_rows],
            x_sem, (step,), head_peer(step),
        )
        for step in range(1, heads)
    ]
    own_kv = qkv.at[pl.ds(1, 2), :, own_columns]
    local_kv = pltpu.make_async_copy(own_kv, kv.at[0, :, p, own_rows], local_sem.at[0])
    local_kv.start()
    ky_copies = {}
    ks_copies = {}

    def spread(step, src):
        dst = kv.at[0, :, p, part_rows(step)]
        for turn in range(1, rows_y):
            ky_copies[turn, step] = send(src, dst, ky_sem, (turn, step), device(z, p_of_y(turn)))
        ks_copies[0, step] = send(src, dst, ks_sem, (0, step), device(z, sibling))

    spread(0, own_kv)
    rate_copies = [
        send(rates.at[p], rates.at[p], rate_sem, (step,), device(z, lax.rem(p + step, plane)))
        for step in range(1, plane)
    ]
    wz_copies = [
        send(w.at[:, z, p], w.at[:, z, p], wz_sem, (step,), device(z_up(step), p))
        for step in range(1, planes)
    ]
    q_copies = [
        send(
            qkv.at[0, :, head_columns(lax.rem(head + step, heads))],
            q.at[own_rows],
            q_sem, (step,), head_peer(step),
        )
        for step in range(1, heads)
    ]
    local_q = pltpu.make_async_copy(qkv.at[0, :, own_columns], q.at[own_rows], local_sem.at[1])
    local_q.start()

    for step in range(1, heads):
        x_copies[step - 1].wait_recv()
        spread(step, kv.at[0, :, p, part_rows(step)])
    local_kv.wait()

    has_next = z + 1 < planes

    def climb(level):
        when = has_next if level == 1 else has_next & (z >= level - 1)
        return send(
            kv.at[level - 1, :, p], kv.at[level, :, p], cz_sem, (level,),
            {"seq": lax.rem(seq + plane, planes * plane), "head": head}, when,
        )

    climbs = {}
    if back >= 1:
        climbs[1] = climb(1)

    for step in range(heads):
        for turn in range(1, rows_y):
            ky_copies[turn, step].wait_recv()
            block = kv.at[0, :, p_of_y(rows_y - turn), part_rows(step)]
            ks_copies[turn, step] = send(block, block, ks_sem, (turn, step), device(z, sibling))

    def relay_in_plane(block, sem_y, sem_s, place, when=None):
        copies = {}
        for turn in range(1, rows_y):
            copies["y", turn] = send(
                block(p), block(p), sem_y, place + (turn,), device(z, p_of_y(turn)), when
            )
        copies["s", 0] = send(block(p), block(p), sem_s, place + (0,), device(z, sibling), when)
        return copies

    def guarded(when, action):
        if when is None:
            action()
        else:
            pl.when(when)(action)

    def relay_to_sibling(copies, block, sem_s, place, when=None):
        for turn in range(1, rows_y):
            guarded(when, copies["y", turn].wait_recv)
            piece = block(p_of_y(rows_y - turn))
            copies["s", turn] = send(piece, piece, sem_s, place + (turn,), device(z, sibling), when)

    def relay_end(copies, when=None):
        for turn in range(rows_y):
            guarded(when, copies["s", turn].wait_recv)

    for copy in wz_copies + rate_copies:
        copy.wait_recv()
    for copy in ks_copies.values():
        copy.wait_recv()

    count = plane * tokens
    key_norm = low(rms_scaled(kv[0, 0].reshape(count, width).astype(jnp.float32)))
    values = kv[0, 1].reshape(count, width)
    rate_row = -jnp.concatenate([rates[index] for index in range(plane)], axis=1)
    column = [low(w[mat, :, p].reshape(planes * state_rows, width)) for mat in range(MATS)]
    gate_act = contract_last(column[0], key_norm)
    up_act = contract_last(column[1], key_norm)
    back_grad = contract_last(column[2], values) * rate_row
    sigmoid_gate = jax.nn.sigmoid(gate_act)
    silu_gate = gate_act * sigmoid_gate
    lefts = (
        lambda: back_grad * up_act * sigmoid_gate * (1.0 + gate_act * (1.0 - sigmoid_gate)),
        lambda: back_grad * silu_gate,
        lambda: silu_gate * up_act * rate_row,
    )
    rs_copies = {}
    for mat in range(MATS):
        total = dot(low(lefts[mat]()), values if mat == 2 else key_norm)
        total = total.reshape(planes, state_rows, width)
        gfull[mat] = total
        gsend[mat] = total.astype(link)
        for step in range(1, planes):
            rs_copies[mat, step] = send(
                gsend.at[mat, z_up(step)], grecv.at[mat, step - 1],
                rs_sem, (mat, step), device(z_up(step), p),
            )

    def w_block(index):
        return w.at[:, :, index]

    def kv_block(level):
        return lambda index: kv.at[level, :, index]

    w_copies = relay_in_plane(w_block, wy_sem, ws_sem, ())

    ctx = {}

    def ctx_in(level):
        when = z >= level
        pl.when(when)(climbs[level].wait_recv)
        ctx[level] = relay_in_plane(kv_block(level), cy_sem, cs_sem, (level,), when)

    if back >= 1:
        ctx_in(1)

    local_q.wait()
    for copy in q_copies:
        copy.wait_recv()

    def attend(level):
        keys = kv[level, 0].reshape(count, width)
        scores = contract_last(q[...], keys) * width ** (-0.5)
        query_pos = p * tokens + lax.broadcasted_iota(jnp.int32, scores.shape, 0)
        key_pos = lax.broadcasted_iota(jnp.int32, scores.shape, 1) - level * count
        visible = (key_pos <= query_pos) & (key_pos > query_pos - WINDOW)
        scores = jnp.where(visible, scores, -jnp.inf)
        row_max = jnp.max(scores, axis=1, keepdims=True)
        context = kv[level, 1].reshape(count, width)
        if level == 0:
            exp_scores = jnp.exp(scores - row_max)
            att_max[...] = row_max
            att_sum[...] = jnp.sum(exp_scores, axis=1, keepdims=True)
            att_acc[...] = dot(low(exp_scores), context)
        else:
            before = att_max[...]
            now = jnp.maximum(before, row_max)
            exp_scores = jnp.exp(scores - now)
            decay = jnp.exp(before - now)
            att_max[...] = now
            att_sum[...] = att_sum[...] * decay + jnp.sum(exp_scores, axis=1, keepdims=True)
            att_acc[...] = att_acc[...] * decay + dot(low(exp_scores), context)

    attend(0)

    gz_copies = {}
    for mat in range(MATS):
        total = gfull[mat, z]
        for step in range(1, planes):
            rs_copies[mat, step].wait_recv()
            total = total + grecv[mat, step - 1].astype(jnp.float32)
        g[mat, z, p] = total.astype(link)
        for step in range(1, planes):
            piece = g.at[mat, z, p]
            gz_copies[mat, step] = send(piece, piece, gz_sem, (mat, step), device(z_up(step), p))

    relay_to_sibling(w_copies, w_block, ws_sem, ())
    if back >= 1:
        relay_to_sibling(ctx[1], kv_block(1), cs_sem, (1,), z >= 1)

    def g_block(mat):
        return lambda index: g.at[mat, :, index]

    g_copies = {}
    for mat in range(MATS):
        for step in range(1, planes):
            gz_copies[mat, step].wait_recv()
        g_copies[mat] = relay_in_plane(g_block(mat), gy_sem, gs_sem, (mat,))

    for level in range(2, back + 1):
        climbs[level] = climb(level)
        if level < back:
            ctx_in(level)
            relay_to_sibling(ctx[level], kv_block(level), cs_sem, (level,), z >= level)

    relay_to_sibling(g_copies[0], g_block(0), gs_sem, (0,))

    def attend_before(level):
        relay_end(ctx[level], z >= level)
        pl.when(z >= level)(functools.partial(attend, level))

    if back >= 1:
        attend_before(1)

    relay_end(w_copies)
    step_size = head_rate[0]

    def orthogonalize(mat):
        full = g[mat].reshape(hidden, width)
        wide = full.astype(jnp.float32)
        scale = 1.0 / (jnp.sqrt(jnp.sum(wide * wide)) + norm_eps)
        gram = contract_last(low(full), low(full)) * (scale * scale)
        iterate = None
        for turn in range(NS_STEPS):
            if turn:
                gram = contract_last(low(iterate), low(iterate))
            gram_low = low(gram)
            poly = low(ns_second * gram + ns_third * dot(gram_low, gram_low))
            if turn:
                iterate = ns_first * iterate + dot(poly, low(iterate))
            else:
                iterate = scale * (ns_first * wide + dot(poly, low(full)))
        moved = step_size * iterate
        direction[...] = moved
        wnew[mat] = low(w[mat].reshape(hidden, width).astype(jnp.float32) - moved)
        own = pl.ds(pl.multiple_of(seq * state_rows, state_rows), state_rows)
        new[mat] = state[mat] - direction[own, :]

    query_norm = low(rms_scaled(q[...].astype(jnp.float32)))
    relay_end(g_copies[0])
    orthogonalize(0)
    relay_to_sibling(g_copies[1], g_block(1), gs_sem, (1,))
    relay_to_sibling(g_copies[2], g_block(2), gs_sem, (2,))
    if back >= 2:
        ctx_in(back)
    gate_q[...] = contract_last(query_norm, wnew[0])
    relay_end(g_copies[1])
    orthogonalize(1)
    if back >= 2:
        relay_to_sibling(ctx[back], kv_block(back), cs_sem, (back,), z >= back)
    gate = gate_q[...]
    active = low(gate * jax.nn.sigmoid(gate) * contract_last(query_norm, wnew[1]))
    relay_end(g_copies[2])
    orthogonalize(2)
    for level in range(2, back + 1):
        attend_before(level)
    comb[...] = low(att_acc[...] / att_sum[...] + dot(active, wnew[2]))

    o_copies = []
    for step in range(1, heads):
        target = lax.rem(head + step, heads)
        rows = pl.ds(pl.multiple_of(target * part, part), part)
        o_copies.append(
            send(comb.at[rows], out.at[:, own_columns], o_sem, (step,), head_peer(step))
        )
    local_out = pltpu.make_async_copy(comb.at[own_rows], out.at[:, own_columns], local_sem.at[0])
    local_out.start()
    local_out.wait()
    for copy in o_copies:
        copy.wait_recv()
    for copy, when in started:
        guarded(when, copy.wait_send)


def shards(sizes, qkv, token_rate, head_rate, fast_state):
    heads, planes, plane, back = sizes
    part, width = qkv.shape[1], qkv.shape[2] // heads
    tokens = token_rate.shape[0]
    state_rows = fast_state.shape[2]
    hidden = state_rows * planes * plane
    rows_y = plane // CORES
    link = jnp.bfloat16 if state_rows % 16 == 0 else jnp.float32
    dma = pltpu.SemaphoreType.DMA
    vmem = pl.BlockSpec(memory_space=pltpu.VMEM)
    combined, new_state = pl.pallas_call(
        functools.partial(kernel, sizes),
        name="block",
        out_shape=(
            jax.ShapeDtypeStruct((part, heads * width), jnp.bfloat16),
            jax.ShapeDtypeStruct((MATS, state_rows, width), jnp.float32),
        ),
        in_specs=[
            pl.BlockSpec(memory_space=pl.ANY), vmem,
            pl.BlockSpec(memory_space=pltpu.SMEM), vmem,
        ],
        out_specs=(vmem, vmem),
        scratch_shapes=[
            pltpu.VMEM((back + 1, 2, plane, tokens, width), jnp.bfloat16),
            pltpu.VMEM((tokens, width), jnp.bfloat16),
            pltpu.VMEM((MATS, planes, plane, state_rows, width), link),
            pltpu.VMEM((MATS, planes, state_rows, width), jnp.float32),
            pltpu.VMEM((MATS, planes, state_rows, width), link),
            pltpu.VMEM((MATS, planes - 1, state_rows, width), link),
            pltpu.VMEM((MATS, planes, plane, state_rows, width), link),
            pltpu.VMEM((MATS, hidden, width), jnp.bfloat16),
            pltpu.VMEM((hidden, width), jnp.float32),
            pltpu.VMEM((plane, 1, tokens), jnp.float32),
            pltpu.VMEM((tokens, width), jnp.bfloat16),
            pltpu.VMEM((tokens, 1), jnp.float32),
            pltpu.VMEM((tokens, 1), jnp.float32),
            pltpu.VMEM((tokens, width), jnp.float32),
            pltpu.VMEM((tokens, hidden), jnp.float32),
            dma((2,)),
            dma((2, heads)),
            dma((2, heads)),
            dma((2, plane)),
            dma((2, rows_y, heads)),
            dma((2, rows_y, heads)),
            dma((2, planes)),
            dma((2, rows_y)),
            dma((2, rows_y)),
            dma((2, MATS, planes)),
            dma((2, MATS, planes)),
            dma((2, MATS, rows_y)),
            dma((2, MATS, rows_y)),
            dma((2, back + 1)),
            dma((2, back + 1, rows_y)),
            dma((2, back + 1, rows_y)),
            dma((2, heads)),
        ],
        compiler_params=pltpu.CompilerParams(
            collective_id=0, has_side_effects=True, vmem_limit_bytes=48 * 1024 * 1024
        ),
    )(qkv, token_rate.reshape(1, tokens), head_rate, fast_state[:, 0])
    return combined, new_state[:, None]


def solution(mesh):
    count, heads = mesh.shape["seq"], mesh.shape["head"]
    plane = CORES
    while plane * plane < count:
        plane *= 2
    planes = count // plane

    def whole(qkv, token_rate, head_rate, fast_state):
        plane_tokens = token_rate.shape[0] // planes
        back = min(-(-(WINDOW - 1) // plane_tokens), planes - 1)
        return jax.shard_map(
            functools.partial(shards, (heads, planes, plane, back)),
            mesh=mesh,
            in_specs=(
                P(None, ("seq", "head"), None),
                P("seq", "head"),
                P("head"),
                P(None, "head", "seq", None),
            ),
            out_specs=(P(("seq", "head"), None), P(None, "head", "seq", None)),
            check_vma=False,
        )(qkv, token_rate, head_rate, fast_state)

    return whole
```

```python
import functools

import jax
import jax.numpy as jnp
from jax import lax
from jax.experimental import pallas as pl
from jax.experimental.pallas import tpu as pltpu
from jax.sharding import PartitionSpec as P

WINDOW = 1024
NS_STEPS = 2

ns_first = 3.4445
ns_second = -4.775
ns_third = 2.0315
rms_eps = 1e-06
norm_eps = 1e-07
lowest = -1e30

MESH = pl.DeviceIdType.MESH
CORES = 2
MATS = 3


def rms_scaled(values):
    return values * lax.rsqrt(jnp.mean(values * values, axis=-1, keepdims=True) + rms_eps)


def contract_last(left_side, right_side):
    return lax.dot_general(
        left_side, right_side, (((1,), (1,)), ((), ())), preferred_element_type=jnp.float32
    )


def low(values):
    return values.astype(jnp.bfloat16)


def dot(left_side, right_side):
    return jnp.dot(left_side, right_side, preferred_element_type=jnp.float32)


def kernel(
    sizes,
    qkv, rate, head_rate, state_hbm,
    out, new,
    state, step_smem, kv, q, q_from, o_send, o_from, l_send, l_from, w,
    gfull, gsend, grecv, g, wnew, direction, rates, comb, own_o, own_l, gate_q,
    local_sem, x_sem, q_sem, rate_sem, ky_sem, ks_sem, wz_sem, wy_sem, ws_sem,
    rs_sem, gz_sem, gy_sem, gs_sem, down_sem, up_sem, log_sem, o_sem,
):
    heads, planes, plane, back = sizes
    rows_y = plane // CORES
    part = qkv.shape[1]
    tokens, width = q.shape
    hidden = direction.shape[0]
    state_rows = state.shape[1]
    link = w.dtype
    count = plane * tokens

    seq = lax.axis_index("seq")
    head = lax.axis_index("head")
    z = seq // plane
    p = lax.rem(seq, plane)
    y = p // CORES
    core = lax.rem(p, CORES)
    sibling = y * CORES + (1 - core)

    def device(z_at, p_at):
        return {"seq": z_at * plane + p_at, "head": head}

    def inside(z_at):
        return (z_at >= 0) & (z_at < planes)

    def wrap(z_at):
        return lax.rem(z_at + 2 * planes, planes)

    def p_of_y(step):
        return lax.rem(y + step, rows_y) * CORES + core

    def head_peer(step):
        return {"seq": seq, "head": lax.rem(head + step, heads)}

    def guarded(when, action):
        if when is None:
            action()
        else:
            pl.when(when)(action)

    peers = [head_peer(step) for step in range(1, heads)]
    peers += [device(z, lax.rem(p + step, plane)) for step in range(1, plane)]
    peers += [device(wrap(z + step), p) for step in range(1, planes)]
    barrier = pltpu.get_barrier_semaphore()
    for peer in peers:
        pl.semaphore_signal(barrier, inc=1, device_id=peer, device_id_type=MESH)

    def local(src, dst, index):
        copy = pltpu.make_async_copy(src, dst, local_sem.at[index])
        copy.start()
        return copy

    state_copy = local(state_hbm, state, 0)
    rate_copy = local(rate, rates.at[p], 1)
    step_copy = local(head_rate, step_smem, 2)

    started = []

    def send(src, dst, sem, place, target, when=None):
        copy = pltpu.make_async_remote_copy(
            src_ref=src,
            dst_ref=dst,
            send_sem=sem.at[(0,) + place],
            recv_sem=sem.at[(1,) + place],
            device_id=target,
            device_id_type=MESH,
        )
        guarded(when, copy.start)
        started.append((copy, when))
        return copy

    def part_rows(step):
        owner = lax.rem(head - step + heads, heads)
        return pl.ds(pl.multiple_of(owner * part, part), part)

    def head_columns(index):
        return pl.ds(pl.multiple_of(index * width, width), width)

    own_rows = part_rows(0)
    own_columns = head_columns(head)
    for level in range(1, back + 1):
        @pl.when(z < level)
        def _(level=level):
            o_from[level - 1] = jnp.zeros_like(o_from[level - 1])
            l_from[level - 1] = jnp.full_like(l_from[level - 1], lowest)
    state_copy.wait()
    for mat in range(MATS):
        w[mat, z, p] = state[mat].astype(link)
    rate_copy.wait()
    step_copy.wait()
    pl.semaphore_wait(barrier, len(peers))

    x_copies = {}
    for kind in range(2):
        for step in range(1, heads):
            x_copies[kind, step] = send(
                qkv.at[1 + kind, :, head_columns(lax.rem(head + step, heads))],
                kv.at[0, kind, p, own_rows],
                x_sem, (kind, step), head_peer(step),
            )
    ky_copies = {}
    ks_copies = {}

    def spread(kind, step, src):
        dst = kv.at[0, kind, p, part_rows(step)]
        for turn in range(1, rows_y):
            ky_copies[turn, kind, step] = send(
                src, dst, ky_sem, (turn, kind, step), device(z, p_of_y(turn))
            )
        ks_copies[0, kind, step] = send(src, dst, ks_sem, (0, kind, step), device(z, sibling))

    for kind in range(2):
        spread(kind, 0, qkv.at[1 + kind, :, own_columns])
    own_kv = qkv.at[pl.ds(1, 2), :, own_columns]
    local_kv = local(own_kv, kv.at[0, :, p, own_rows], 0)

    ways = (1, -1)

    def z_spread(block, sem, place, distance, way_index):
        way = ways[way_index]
        piece = block(wrap(z - way * distance))
        for jump in (2, 1):
            if distance + jump < planes:
                when = inside(z - way * distance) & inside(z + way * jump)
                copies = send(
                    piece, piece, sem, place + (way_index, distance + jump),
                    device(wrap(z + way * jump), p), when,
                )
                yield (way_index, distance + jump), copies

    def z_start(block, sem, place):
        copies = {}
        for way_index in range(2):
            copies.update(z_spread(block, sem, place, 0, way_index))
        return copies

    def z_wait(copies, way_index, distance):
        when = inside(z - ways[way_index] * distance)
        pl.when(when)(copies[way_index, distance].wait_recv)

    def z_relay(copies, block, sem, place):
        for distance in range(2, planes - 1, 2):
            for way_index in range(2):
                z_wait(copies, way_index, distance)
                copies.update(z_spread(block, sem, place, distance, way_index))

    def z_end(copies):
        relayed = range(2, planes - 1, 2)
        for distance in range(1, planes):
            if distance not in relayed:
                for way_index in range(2):
                    z_wait(copies, way_index, distance)

    def w_piece(z_at):
        return w.at[:, z_at, p]

    wz_copies = z_start(w_piece, wz_sem, ())
    rate_copies = [
        send(rates.at[p], rates.at[p], rate_sem, (step,), device(z, lax.rem(p + step, plane)))
        for step in range(1, plane)
    ]
    q_copies = [
        send(
            qkv.at[0, :, head_columns(lax.rem(head + step, heads))],
            q.at[own_rows],
            q_sem, (step,), head_peer(step),
        )
        for step in range(1, heads)
    ]
    local_q = local(qkv.at[0, :, own_columns], q.at[own_rows], 1)

    for kind in range(2):
        for step in range(1, heads):
            x_copies[kind, step].wait_recv()
            spread(kind, step, kv.at[0, kind, p, part_rows(step)])
    local_kv.wait()
    z_relay(wz_copies, w_piece, wz_sem, ())

    local_q.wait()
    for copy in q_copies:
        copy.wait_recv()

    downs = {}

    def descend(level):
        src = q if level == 1 else q_from.at[level - 2]
        when = (z >= 1) & (z + level - 1 < planes)
        downs[level] = send(
            src, q_from.at[level - 1], down_sem, (level,), device(wrap(z - 1), p), when
        )

    if back >= 1:
        descend(1)

    for kind in range(2):
        for step in range(heads):
            for turn in range(1, rows_y):
                ky_copies[turn, kind, step].wait_recv()
                block = kv.at[0, kind, p_of_y(rows_y - turn), part_rows(step)]
                ks_copies[turn, kind, step] = send(
                    block, block, ks_sem, (turn, kind, step), device(z, sibling)
                )

    def relay_in_plane(block, sem_y, sem_s, place):
        copies = {}
        for turn in range(1, rows_y):
            copies["y", turn] = send(
                block(p), block(p), sem_y, place + (turn,), device(z, p_of_y(turn))
            )
        copies["s", 0] = send(block(p), block(p), sem_s, place + (0,), device(z, sibling))
        return copies

    def relay_to_sibling(copies, block, sem_s, place):
        for turn in range(1, rows_y):
            copies["y", turn].wait_recv()
            piece = block(p_of_y(rows_y - turn))
            copies["s", turn] = send(piece, piece, sem_s, place + (turn,), device(z, sibling))

    def relay_end(copies):
        for turn in range(rows_y):
            copies["s", turn].wait_recv()

    z_end(wz_copies)
    for copy in rate_copies:
        copy.wait_recv()
    for copy in ks_copies.values():
        copy.wait_recv()

    keys = kv[0, 0].reshape(count, width)
    values = kv[0, 1].reshape(count, width)
    key_norm = low(rms_scaled(keys.astype(jnp.float32)))
    rate_row = -jnp.concatenate([rates[index] for index in range(plane)], axis=1)
    column = [low(w[mat, :, p].reshape(planes * state_rows, width)) for mat in range(MATS)]
    gate_act = contract_last(column[0], key_norm)
    up_act = contract_last(column[1], key_norm)
    back_grad = contract_last(column[2], values) * rate_row
    sigmoid_gate = jax.nn.sigmoid(gate_act)
    silu_gate = gate_act * sigmoid_gate
    lefts = (
        lambda: back_grad * up_act * sigmoid_gate * (1.0 + gate_act * (1.0 - sigmoid_gate)),
        lambda: back_grad * silu_gate,
        lambda: silu_gate * up_act * rate_row,
    )

    rs_copies = {}

    def rs_send(mat, way_index, distance):
        way = ways[way_index]
        jump = 2 - distance % 2
        owner = wrap(z + way * distance)
        rs_copies[mat, way_index, distance] = send(
            gsend.at[mat, owner], grecv.at[mat, way_index, distance - 1],
            rs_sem, (mat, way_index, distance), device(wrap(z + way * jump), p),
            inside(z + way * distance),
        )

    def rs_collect(mat, way_index, distance):
        way = ways[way_index]
        owner = wrap(z + way * distance)
        for behind in (1, 2):
            if distance + behind < planes:
                @pl.when(inside(z + way * distance) & inside(z - way * behind))
                def _(behind=behind):
                    rs_copies[mat, way_index, distance + behind].wait_recv()
                    gfull[mat, owner] = gfull[mat, owner] + grecv[
                        mat, way_index, distance + behind - 1
                    ].astype(jnp.float32)
        if 0 < distance < planes - 1:
            @pl.when(inside(z + way * distance) & inside(z - way))
            def _():
                gsend[mat, owner] = gfull[mat, owner].astype(link)

    for mat in range(MATS):
        total = dot(low(lefts[mat]()), values if mat == 2 else key_norm)
        total = total.reshape(planes, state_rows, width)
        gfull[mat] = total
        gsend[mat] = total.astype(link)
        for distance in range(planes - 1, 0, -1):
            if distance % 2:
                for way_index in range(2):
                    rs_send(mat, way_index, distance)

    for level in range(2, back + 1):
        pl.when(z + level - 1 < planes)(downs[level - 1].wait_recv)
        descend(level)

    def attend(level):
        queries = q[...] if level == 0 else q_from[level - 1]
        scores = contract_last(queries, kv[0, 0].reshape(count, width)) * width ** (-0.5)
        query_pos = level * count + p * tokens + lax.broadcasted_iota(jnp.int32, scores.shape, 0)
        key_pos = lax.broadcasted_iota(jnp.int32, scores.shape, 1)
        visible = (key_pos <= query_pos) & (key_pos > query_pos - WINDOW)
        scores = jnp.where(visible, scores, -jnp.inf)
        row_max = jnp.maximum(jnp.max(scores, axis=1, keepdims=True), lowest)
        exp_scores = jnp.exp(scores - row_max)
        row_sum = jnp.sum(exp_scores, axis=1, keepdims=True)
        result = dot(low(exp_scores), kv[0, 1].reshape(count, width))
        result = result / jnp.maximum(row_sum, 1e-30)
        log_sum = jnp.where(row_sum > 0.0, row_max + jnp.log(jnp.maximum(row_sum, 1e-30)), lowest)
        if level == 0:
            own_o[...] = result
            own_l[...] = log_sum
        else:
            o_send[level - 1] = low(result)
            l_send[level - 1] = jnp.broadcast_to(log_sum, (tokens, tokens)).T[:1]

    for mat in range(MATS):
        for distance in range(planes - 2 + planes % 2, 0, -2):
            for way_index in range(2):
                rs_collect(mat, way_index, distance)
                rs_send(mat, way_index, distance)

    w_copies = relay_in_plane(lambda index: w.at[:, :, index], wy_sem, ws_sem, ())
    attend(0)

    def g_piece(mat):
        return lambda z_at: g.at[mat, z_at, p]

    gz_copies = {}
    for mat in range(MATS):
        for way_index in range(2):
            rs_collect(mat, way_index, 0)
        g[mat, z, p] = gfull[mat, z].astype(link)
        gz_copies[mat] = z_start(g_piece(mat), gz_sem, (mat,))

    relay_to_sibling(w_copies, lambda index: w.at[:, :, index], ws_sem, ())

    ups = {}
    for level in range(back, 0, -1):
        when = z + level < planes

        @pl.when(when)
        def _(level=level):
            if level == back:
                downs[level].wait_recv()
            attend(level)

    for mat in range(MATS):
        z_relay(gz_copies[mat], g_piece(mat), gz_sem, (mat,))
    for level in range(back, 0, -1):
        when = z + level < planes
        target = device(wrap(z + level), p)
        ups[level] = (
            send(o_send.at[level - 1], o_from.at[level - 1], up_sem, (level,), target, when),
            send(l_send.at[level - 1], l_from.at[level - 1], log_sem, (level,), target, when),
        )

    def g_block(mat):
        return lambda index: g.at[mat, :, index]

    g_copies = {}
    for mat in range(MATS):
        z_end(gz_copies[mat])
        g_copies[mat] = relay_in_plane(g_block(mat), gy_sem, gs_sem, (mat,))
        if mat:
            relay_to_sibling(g_copies[mat - 1], g_block(mat - 1), gs_sem, (mat - 1,))

    relay_end(w_copies)
    step_size = step_smem[0]

    def orthogonalize(mat):
        full = g[mat].reshape(hidden, width)
        wide = full.astype(jnp.float32)
        scale = 1.0 / (jnp.sqrt(jnp.sum(wide * wide)) + norm_eps)
        gram = contract_last(low(full), low(full)) * (scale * scale)
        iterate = None
        for turn in range(NS_STEPS):
            if turn:
                gram = contract_last(low(iterate), low(iterate))
            gram_low = low(gram)
            poly = low(ns_second * gram + ns_third * dot(gram_low, gram_low))
            if turn:
                iterate = ns_first * iterate + dot(poly, low(iterate))
            else:
                iterate = scale * (ns_first * wide + dot(poly, low(full)))
        moved = step_size * iterate
        direction[...] = moved
        wnew[mat] = low(w[mat].reshape(hidden, width).astype(jnp.float32) - moved)
        own = pl.ds(pl.multiple_of(seq * state_rows, state_rows), state_rows)
        new[mat] = state[mat] - direction[own, :]

    query_norm = low(rms_scaled(q[...].astype(jnp.float32)))
    relay_end(g_copies[0])
    orthogonalize(0)
    relay_to_sibling(g_copies[2], g_block(2), gs_sem, (2,))
    gate_q[...] = contract_last(query_norm, wnew[0])
    relay_end(g_copies[1])
    orthogonalize(1)
    gate = gate_q[...]
    active = low(gate * jax.nn.sigmoid(gate) * contract_last(query_norm, wnew[1]))
    for level in range(1, back + 1):
        for copy in ups[level]:
            pl.when(z >= level)(copy.wait_recv)
    logs = [own_l[...]]
    for level in range(1, back + 1):
        row = jnp.broadcast_to(l_from[level - 1], (tokens, tokens))
        logs.append(row.T[:, :1])
    top = functools.reduce(jnp.maximum, logs)
    shares = [jnp.exp(log - top) for log in logs]
    attention = shares[0] * own_o[...]
    for level in range(1, back + 1):
        attention = attention + shares[level] * o_from[level - 1].astype(jnp.float32)
    own_o[...] = attention / functools.reduce(jnp.add, shares)
    relay_end(g_copies[2])
    orthogonalize(2)
    comb[...] = low(own_o[...] + dot(active, wnew[2]))

    o_copies = []
    for step in range(1, heads):
        target = lax.rem(head + step, heads)
        rows = pl.ds(pl.multiple_of(target * part, part), part)
        o_copies.append(
            send(comb.at[rows], out.at[:, own_columns], o_sem, (step,), head_peer(step))
        )
    local_out = local(comb.at[own_rows], out.at[:, own_columns], 0)
    local_out.wait()
    for copy in o_copies:
        copy.wait_recv()
    for copy, when in started:
        guarded(when, copy.wait_send)


def shards(sizes, qkv, token_rate, head_rate, fast_state):
    heads, planes, plane, back = sizes
    part, width = qkv.shape[1], qkv.shape[2] // heads
    tokens = token_rate.shape[0]
    state_rows = fast_state.shape[2]
    hidden = state_rows * planes * plane
    rows_y = plane // CORES
    levels = max(back, 1)
    link = jnp.bfloat16 if state_rows % 16 == 0 else jnp.float32
    dma = pltpu.SemaphoreType.DMA
    vmem = pl.BlockSpec(memory_space=pltpu.VMEM)
    combined, new_state = pl.pallas_call(
        functools.partial(kernel, sizes),
        name="block",
        out_shape=(
            jax.ShapeDtypeStruct((part, heads * width), jnp.bfloat16),
            jax.ShapeDtypeStruct((MATS, state_rows, width), jnp.float32),
        ),
        in_specs=[pl.BlockSpec(memory_space=pltpu.HBM)] * 4,
        out_specs=(vmem, vmem),
        scratch_shapes=[
            pltpu.VMEM((MATS, state_rows, width), jnp.float32),
            pltpu.SMEM((1,), jnp.float32),
            pltpu.VMEM((1, 2, plane, tokens, width), jnp.bfloat16),
            pltpu.VMEM((tokens, width), jnp.bfloat16),
            pltpu.VMEM((levels, tokens, width), jnp.bfloat16),
            pltpu.VMEM((levels, tokens, width), jnp.bfloat16),
            pltpu.VMEM((levels, tokens, width), jnp.bfloat16),
            pltpu.VMEM((levels, 1, tokens), jnp.float32),
            pltpu.VMEM((levels, 1, tokens), jnp.float32),
            pltpu.VMEM((MATS, planes, plane, state_rows, width), link),
            pltpu.VMEM((MATS, planes, state_rows, width), jnp.float32),
            pltpu.VMEM((MATS, planes, state_rows, width), link),
            pltpu.VMEM((MATS, 2, planes - 1, state_rows, width), link),
            pltpu.VMEM((MATS, planes, plane, state_rows, width), link),
            pltpu.VMEM((MATS, hidden, width), jnp.bfloat16),
            pltpu.VMEM((hidden, width), jnp.float32),
            pltpu.VMEM((plane, 1, tokens), jnp.float32),
            pltpu.VMEM((tokens, width), jnp.bfloat16),
            pltpu.VMEM((tokens, width), jnp.float32),
            pltpu.VMEM((tokens, 1), jnp.float32),
            pltpu.VMEM((tokens, hidden), jnp.float32),
            dma((3,)),
            dma((2, 2, heads)),
            dma((2, heads)),
            dma((2, plane)),
            dma((2, rows_y, 2, heads)),
            dma((2, rows_y, 2, heads)),
            dma((2, 2, planes)),
            dma((2, rows_y)),
            dma((2, rows_y)),
            dma((2, MATS, 2, planes)),
            dma((2, MATS, 2, planes)),
            dma((2, MATS, rows_y)),
            dma((2, MATS, rows_y)),
            dma((2, back + 1)),
            dma((2, back + 1)),
            dma((2, back + 1)),
            dma((2, heads)),
        ],
        compiler_params=pltpu.CompilerParams(
            collective_id=0, has_side_effects=True, vmem_limit_bytes=48 * 1024 * 1024
        ),
    )(qkv, token_rate.reshape(1, tokens), head_rate, fast_state[:, 0])
    return combined, new_state[:, None]


def solution(mesh):
    count, heads = mesh.shape["seq"], mesh.shape["head"]
    plane = CORES
    while plane * plane < count:
        plane *= 2
    planes = count // plane

    def whole(qkv, token_rate, head_rate, fast_state):
        plane_tokens = token_rate.shape[0] // planes
        back = min(-(-(WINDOW - 1) // plane_tokens), planes - 1)
        return jax.shard_map(
            functools.partial(shards, (heads, planes, plane, back)),
            mesh=mesh,
            in_specs=(
                P(None, ("seq", "head"), None),
                P("seq", "head"),
                P("head"),
                P(None, "head", "seq", None),
            ),
            out_specs=(P(("seq", "head"), None), P(None, "head", "seq", None)),
            check_vma=False,
        )(qkv, token_rate, head_rate, fast_state)

    return whole
```

```python
import functools

import jax
import jax.numpy as jnp
from jax import lax
from jax.experimental import pallas as pl
from jax.experimental.pallas import tpu as pltpu
from jax.sharding import PartitionSpec as P

WINDOW = 1024
NS_STEPS = 2

ns_first = 3.4445
ns_second = -4.775
ns_third = 2.0315
rms_eps = 1e-06
norm_eps = 1e-07
lowest = -1e30

MESH = pl.DeviceIdType.MESH
CORES = 2
MATS = 3
ORDER = (0, 2, 1)
SHARED = 1


def rms_scaled(values):
    return values * lax.rsqrt(jnp.mean(values * values, axis=-1, keepdims=True) + rms_eps)


def contract_last(left_side, right_side):
    return lax.dot_general(
        left_side, right_side, (((1,), (1,)), ((), ())), preferred_element_type=jnp.float32
    )


def low(values):
    return values.astype(jnp.bfloat16)


def dot(left_side, right_side):
    return jnp.dot(left_side, right_side, preferred_element_type=jnp.float32)


def kernel(
    sizes,
    qkv, rate, head_rate, state_hbm,
    out, new,
    state, step_smem, moved, new_rows, kv, q, q_from, o_send, o_from, l_send, l_from, w,
    gfull, gsend, grecv, g, wnew, direction, rates, comb, own_o, own_l,
    local_sem, q_sem, rate_sem, ky_sem, ks_sem, wz_sem, wy_sem, ws_sem,
    rs_sem, gz_sem, gy_sem, gs_sem, down_sem, up_sem, log_sem, o_sem, fresh_sem,
):
    heads, planes, plane, back = sizes
    rows_y = plane // CORES
    part = qkv.shape[1]
    tokens, width = q.shape
    hidden = direction.shape[1]
    state_rows = state.shape[1]
    link = w.dtype
    count = plane * tokens

    seq = lax.axis_index("seq")
    head = lax.axis_index("head")
    z = seq // plane
    p = lax.rem(seq, plane)
    y = p // CORES
    core = lax.rem(p, CORES)
    sibling = y * CORES + (1 - core)

    def device(z_at, p_at):
        return {"seq": z_at * plane + p_at, "head": head}

    def inside(z_at):
        return (z_at >= 0) & (z_at < planes)

    def wrap(z_at):
        return lax.rem(z_at + 2 * planes, planes)

    def p_of_y(step):
        return lax.rem(y + step, rows_y) * CORES + core

    def head_peer(step):
        return {"seq": seq, "head": lax.rem(head + step, heads)}

    def guarded(when, action):
        if when is None:
            action()
        else:
            pl.when(when)(action)

    def far_peer(turn, step):
        return {"seq": z * plane + p_of_y(turn), "head": lax.rem(head + step, heads)}

    far = [(turn, step) for turn in range(rows_y) for step in range(heads) if turn + step]
    peers = [far_peer(turn, step) for turn, step in far if step]
    peers += [device(z, lax.rem(p + step, plane)) for step in range(1, plane)]
    peers += [device(wrap(z + step), p) for step in range(1, planes)]
    barrier = pltpu.get_barrier_semaphore()
    for peer in peers:
        pl.semaphore_signal(barrier, inc=1, device_id=peer, device_id_type=MESH)

    def local(src, dst, index):
        copy = pltpu.make_async_copy(src, dst, local_sem.at[index])
        copy.start()
        return copy

    state_copy = local(state_hbm, state, 0)
    rate_copy = local(rate, rates.at[p], 1)
    step_copy = local(head_rate, step_smem, 2)

    started = []

    def send(src, dst, sem, place, target, when=None):
        copy = pltpu.make_async_remote_copy(
            src_ref=src,
            dst_ref=dst,
            send_sem=sem.at[(0,) + place],
            recv_sem=sem.at[(1,) + place],
            device_id=target,
            device_id_type=MESH,
        )
        guarded(when, copy.start)
        started.append((copy, when))
        return copy

    def part_rows(step):
        owner = lax.rem(head - step + heads, heads)
        return pl.ds(pl.multiple_of(owner * part, part), part)

    def head_columns(index):
        return pl.ds(pl.multiple_of(index * width, width), width)

    own_rows = part_rows(0)
    own_columns = head_columns(head)
    for level in range(1, back + 1):
        @pl.when(z < level)
        def _(level=level):
            o_from[level - 1] = jnp.zeros_like(o_from[level - 1])
            l_from[level - 1] = jnp.full_like(l_from[level - 1], lowest)
    pl.semaphore_wait(barrier, len(peers))

    k_copies = {}
    for turn, step in far[::-1]:
        k_copies[turn, step] = send(
            qkv.at[pl.ds(1, 2), :, head_columns(lax.rem(head + step, heads))],
            kv.at[0, :, p, own_rows],
            ky_sem, (turn, step), far_peer(turn, step),
        )
    own_kv = qkv.at[pl.ds(1, 2), :, own_columns]
    ks_copies = {
        (0, 0): send(own_kv, kv.at[0, :, p, own_rows], ks_sem, (0, 0), device(z, sibling))
    }
    local_kv = local(own_kv, kv.at[0, :, p, own_rows], 3)
    local_q = local(qkv.at[0, :, own_columns], q.at[own_rows], 4)
    state_copy.wait()
    for place, mat in enumerate(ORDER):
        w[place, z, p] = state[mat].astype(link)

    ways = (1, -1)

    def z_spread(block, sem, place, distance, way_index):
        way = ways[way_index]
        piece = block(wrap(z - way * distance))
        for jump in (2, 1):
            if distance + jump < planes:
                when = inside(z - way * distance) & inside(z + way * jump)
                copies = send(
                    piece, piece, sem, place + (way_index, distance + jump),
                    device(wrap(z + way * jump), p), when,
                )
                yield (way_index, distance + jump), copies

    def z_start(block, sem, place):
        copies = {}
        for way_index in range(2):
            copies.update(z_spread(block, sem, place, 0, way_index))
        return copies

    def z_wait(copies, way_index, distance):
        when = inside(z - ways[way_index] * distance)
        pl.when(when)(copies[way_index, distance].wait_recv)

    def z_relay(copies, block, sem, place):
        for distance in range(2, planes - 1, 2):
            for way_index in range(2):
                z_wait(copies, way_index, distance)
                copies.update(z_spread(block, sem, place, distance, way_index))

    def z_end(copies):
        relayed = range(2, planes - 1, 2)
        for distance in range(1, planes):
            if distance not in relayed:
                for way_index in range(2):
                    z_wait(copies, way_index, distance)

    def w_piece(z_at):
        return w.at[:, z_at, p]

    wz_copies = z_start(w_piece, wz_sem, ())
    rate_copy.wait()
    rate_copies = [
        send(rates.at[p], rates.at[p], rate_sem, (step,), device(z, lax.rem(p + step, plane)))
        for step in range(1, plane)
    ]
    for step in range(1, heads):
        k_copies[0, step].wait_recv()
    q_copies = [
        send(
            qkv.at[0, :, head_columns(lax.rem(head + step, heads))],
            q.at[own_rows],
            q_sem, (step,), head_peer(step),
        )
        for step in range(1, heads)
    ]
    for turn, step in far:
        if turn:
            k_copies[turn, step].wait_recv()
        block = kv.at[0, :, p_of_y(rows_y - turn), part_rows(step)]
        ks_copies[turn, step] = send(block, block, ks_sem, (turn, step), device(z, sibling))
    z_relay(wz_copies, w_piece, wz_sem, ())

    local_q.wait()
    for copy in q_copies:
        copy.wait_recv()

    downs = {}

    def descend(level):
        src = q if level == 1 else q_from.at[level - 2]
        when = (z >= 1) & (z + level - 1 < planes)
        downs[level] = send(
            src, q_from.at[level - 1], down_sem, (level,), device(wrap(z - 1), p), when
        )

    if back >= 1:
        descend(1)

    for_sibling = pl.ds(1 - core, 2)

    def plane_send(block, sem_y, sem_s, place, when=None):
        copies = {}
        for turn in range(1, rows_y):
            copies["y", turn] = send(
                block(slice(None), p), block(slice(None), p), sem_y, (turn,) + place,
                device(z, p_of_y(turn)), when,
            )
        copies["s", 0] = send(
            block(for_sibling, p), block(for_sibling, p), sem_s, (0,) + place,
            device(z, sibling), when,
        )
        return copies

    def plane_relay(copies, block, sem_s, place, when=None):
        for turn in range(1, rows_y):
            guarded(when, copies["y", turn].wait_recv)
            piece = block(for_sibling, p_of_y(rows_y - turn))
            copies["s", turn] = send(
                piece, piece, sem_s, (turn,) + place, device(z, sibling), when
            )

    def plane_end(copies, when=None):
        for turn in range(rows_y):
            guarded(when, copies["s", turn].wait_recv)

    local_kv.wait()
    z_end(wz_copies)
    for copy in rate_copies:
        copy.wait_recv()
    for copy in ks_copies.values():
        copy.wait_recv()

    keys = kv[0, 0].reshape(count, width)
    values = kv[0, 1].reshape(count, width)
    key_norm = low(rms_scaled(keys.astype(jnp.float32)))
    rate_row = -jnp.concatenate([rates[index] for index in range(plane)], axis=1)
    column = [
        low(w[place, :, p].reshape(planes * state_rows, width)) for place in range(MATS)
    ]
    gate_act = contract_last(column[0], key_norm)
    up_act = contract_last(column[2], key_norm)
    back_grad = contract_last(column[1], values) * rate_row
    sigmoid_gate = jax.nn.sigmoid(gate_act)
    silu_gate = gate_act * sigmoid_gate
    lefts = (
        back_grad * up_act * sigmoid_gate * (1.0 + gate_act * (1.0 - sigmoid_gate)),
        silu_gate * up_act * rate_row,
        back_grad * silu_gate,
    )
    for place in range(MATS):
        total = dot(low(lefts[place]), values if place == SHARED else key_norm)
        total = total.reshape(planes, state_rows, width)
        gfull[place] = total
        gsend[place] = total.astype(link)
    rs_copies = [
        send(
            gsend.at[:, wrap(z + step)], grecv.at[:, step - 1],
            rs_sem, (step,), device(wrap(z + step), p),
        )
        for step in range(1, planes)
    ]

    def attend(level):
        queries = q[...] if level == 0 else q_from[level - 1]
        scores = contract_last(queries, kv[0, 0].reshape(count, width)) * width ** (-0.5)
        query_pos = level * count + p * tokens + lax.broadcasted_iota(jnp.int32, scores.shape, 0)
        key_pos = lax.broadcasted_iota(jnp.int32, scores.shape, 1)
        visible = (key_pos <= query_pos) & (key_pos > query_pos - WINDOW)
        scores = jnp.where(visible, scores, -jnp.inf)
        row_max = jnp.maximum(jnp.max(scores, axis=1, keepdims=True), lowest)
        exp_scores = jnp.exp(scores - row_max)
        row_sum = jnp.sum(exp_scores, axis=1, keepdims=True)
        result = dot(low(exp_scores), kv[0, 1].reshape(count, width))
        result = result / jnp.maximum(row_sum, 1e-30)
        log_sum = jnp.where(row_sum > 0.0, row_max + jnp.log(jnp.maximum(row_sum, 1e-30)), lowest)
        if level == 0:
            own_o[...] = result
            own_l[...] = log_sum
        else:
            o_send[level - 1] = low(result)
            l_send[level - 1] = jnp.broadcast_to(log_sum, (tokens, tokens)).T[:1]

    def w_block(places, index):
        return w.at[places, :, index]

    w_copies = plane_send(w_block, wy_sem, ws_sem, ())
    attend(0)

    def attend_for(level):
        @pl.when(z + level < planes)
        def _():
            downs[level].wait_recv()
            attend(level)

    ups = {}

    def ascend(level):
        when = z + level < planes
        target = device(wrap(z + level), p)
        ups[level] = (
            send(o_send.at[level - 1], o_from.at[level - 1], up_sem, (level,), target, when),
            send(l_send.at[level - 1], l_from.at[level - 1], log_sem, (level,), target, when),
        )

    if back >= 1:
        attend_for(1)

    total = gfull[:, z]
    for step in range(1, planes):
        rs_copies[step - 1].wait_recv()
        total = total + grecv[:, step - 1].astype(jnp.float32)
    g[:, z, p] = total.astype(link)

    def g_piece(z_at):
        return g.at[:, z_at, p]

    gz_copies = z_start(g_piece, gz_sem, ())

    def g_block(way_index, distance):
        z_at = wrap(z - ways[way_index] * distance)
        return lambda places, index: g.at[places, z_at, index]

    def g_when(way_index, distance):
        return inside(z - ways[way_index] * distance) if distance else None

    def g_ways(distance):
        return range(2 if distance else 1)

    g_copies = {}

    def g_forward(distance):
        for way_index in g_ways(distance):
            key = (way_index, distance)
            when = g_when(*key)
            if distance:
                pl.when(when)(gz_copies[key].wait_recv)
                if distance % 2 == 0:
                    gz_copies.update(z_spread(g_piece, gz_sem, (), distance, way_index))
            g_copies[key] = plane_send(g_block(*key), gy_sem, gs_sem, key, when)

    def g_relay(distance):
        for way_index in g_ways(distance):
            key = (way_index, distance)
            plane_relay(g_copies[key], g_block(*key), gs_sem, key, g_when(*key))

    g_forward(0)
    if back >= 2:
        descend(2)
    if back >= 1:
        ascend(1)
    plane_relay(w_copies, w_block, ws_sem, ())
    for distance in range(1, planes):
        g_forward(distance)
        g_relay(distance - 1)
        if distance == planes - 2:
            for level in range(2, back + 1):
                attend_for(level)
                ascend(level)
                if level < back:
                    descend(level + 1)
    query_norm = low(rms_scaled(q[...].astype(jnp.float32)))
    g_relay(planes - 1)
    plane_end(w_copies)
    for key, copies in g_copies.items():
        plane_end(copies, g_when(*key))

    step_copy.wait()
    step_size = step_smem[0]
    own = pl.ds(pl.multiple_of(seq * state_rows, state_rows), state_rows)

    def orthogonalize(place, mat, slot):
        full = g[place].reshape(hidden, width)
        wide = full.astype(jnp.float32)
        scale = 1.0 / (jnp.sqrt(jnp.sum(wide * wide)) + norm_eps)
        gram = contract_last(low(full), low(full)) * (scale * scale)
        iterate = None
        for turn in range(NS_STEPS):
            if turn:
                gram = contract_last(low(iterate), low(iterate))
            gram_low = low(gram)
            poly = low(ns_second * gram + ns_third * dot(gram_low, gram_low))
            if turn:
                iterate = ns_first * iterate + dot(poly, low(iterate))
            else:
                iterate = scale * (ns_first * wide + dot(poly, low(full)))
        change = step_size * iterate
        direction[slot] = change
        wnew[place] = low(w[place].reshape(hidden, width).astype(jnp.float32) - change)
        new_rows[mat] = state[mat] - direction[slot, own, :]

    orthogonalize(2 * core, core, 0)
    sibling_seq = z * plane + sibling
    theirs = pl.ds(pl.multiple_of(sibling_seq * state_rows, state_rows), state_rows)
    swaps = [
        send(wnew.at[2 * core], wnew.at[2 * core], fresh_sem, (0,), device(z, sibling)),
        send(direction.at[0, theirs], moved, fresh_sem, (1,), device(z, sibling)),
    ]
    orthogonalize(SHARED, ORDER[SHARED], 1)
    for level in range(1, back + 1):
        for copy in ups[level]:
            pl.when(z >= level)(copy.wait_recv)
    logs = [own_l[...]]
    for level in range(1, back + 1):
        row = jnp.broadcast_to(l_from[level - 1], (tokens, tokens))
        logs.append(row.T[:, :1])
    top = functools.reduce(jnp.maximum, logs)
    shares = [jnp.exp(log - top) for log in logs]
    attention = shares[0] * own_o[...]
    for level in range(1, back + 1):
        attention = attention + shares[level] * o_from[level - 1].astype(jnp.float32)
    attention = attention / functools.reduce(jnp.add, shares)
    for copy in swaps:
        copy.wait_recv()
    new_rows[1 - core] = state[1 - core] - moved[...]
    local_new = local(new_rows, new, 1)
    gate = contract_last(query_norm, wnew[0])
    active = low(gate * jax.nn.sigmoid(gate) * contract_last(query_norm, wnew[2]))
    comb[...] = low(attention + dot(active, wnew[SHARED]))

    o_copies = []
    for step in range(1, heads):
        target = lax.rem(head + step, heads)
        rows = pl.ds(pl.multiple_of(target * part, part), part)
        o_copies.append(
            send(comb.at[rows], out.at[:, own_columns], o_sem, (step,), head_peer(step))
        )
    local_out = local(comb.at[own_rows], out.at[:, own_columns], 0)
    local_out.wait()
    local_new.wait()
    for copy in o_copies:
        copy.wait_recv()
    for copy, when in started:
        guarded(when, copy.wait_send)


def hand_over(combined, new_state, combined_out, new_state_out, sems):
    first = pltpu.make_async_copy(combined, combined_out, sems.at[0])
    second = pltpu.make_async_copy(new_state, new_state_out, sems.at[1])
    first.start()
    second.start()
    first.wait()
    second.wait()


def held(values):
    return pltpu.with_memory_space_constraint(values, pltpu.HBM)


def shards(sizes, qkv, token_rate, head_rate, fast_state):
    heads, planes, plane, back = sizes
    part, width = qkv.shape[1], qkv.shape[2] // heads
    tokens = token_rate.shape[0]
    state_rows = fast_state.shape[2]
    hidden = state_rows * planes * plane
    rows_y = plane // CORES
    levels = max(back, 1)
    link = jnp.bfloat16 if state_rows % 16 == 0 else jnp.float32
    dma = pltpu.SemaphoreType.DMA
    hbm = pl.BlockSpec(memory_space=pltpu.HBM)
    combined, new_state = pl.pallas_call(
        functools.partial(kernel, sizes),
        name="block",
        out_shape=(
            jax.ShapeDtypeStruct((part, heads * width), jnp.bfloat16),
            jax.ShapeDtypeStruct((MATS, state_rows, width), jnp.float32),
        ),
        in_specs=[hbm] * 4,
        out_specs=(hbm, hbm),
        scratch_shapes=[
            pltpu.VMEM((MATS, state_rows, width), jnp.float32),
            pltpu.SMEM((1,), jnp.float32),
            pltpu.VMEM((state_rows, width), jnp.float32),
            pltpu.VMEM((MATS, state_rows, width), jnp.float32),
            pltpu.VMEM((1, 2, plane, tokens, width), jnp.bfloat16),
            pltpu.VMEM((tokens, width), jnp.bfloat16),
            pltpu.VMEM((levels, tokens, width), jnp.bfloat16),
            pltpu.VMEM((levels, tokens, width), jnp.bfloat16),
            pltpu.VMEM((levels, tokens, width), jnp.bfloat16),
            pltpu.VMEM((levels, 1, tokens), jnp.float32),
            pltpu.VMEM((levels, 1, tokens), jnp.float32),
            pltpu.VMEM((MATS, planes, plane, state_rows, width), link),
            pltpu.VMEM((MATS, planes, state_rows, width), jnp.float32),
            pltpu.VMEM((MATS, planes, state_rows, width), link),
            pltpu.VMEM((MATS, planes - 1, state_rows, width), link),
            pltpu.VMEM((MATS, planes, plane, state_rows, width), link),
            pltpu.VMEM((MATS, hidden, width), jnp.bfloat16),
            pltpu.VMEM((2, hidden, width), jnp.float32),
            pltpu.VMEM((plane, 1, tokens), jnp.float32),
            pltpu.VMEM((tokens, width), jnp.bfloat16),
            pltpu.VMEM((tokens, width), jnp.float32),
            pltpu.VMEM((tokens, 1), jnp.float32),
            dma((5,)),
            dma((2, heads)),
            dma((2, plane)),
            dma((2, rows_y, heads)),
            dma((2, rows_y, heads)),
            dma((2, 2, planes)),
            dma((2, rows_y)),
            dma((2, rows_y)),
            dma((2, planes)),
            dma((2, 2, planes)),
            dma((2, rows_y, 2, planes)),
            dma((2, rows_y, 2, planes)),
            dma((2, back + 1)),
            dma((2, back + 1)),
            dma((2, back + 1)),
            dma((2, heads)),
            dma((2, 2)),
        ],
        compiler_params=pltpu.CompilerParams(
            collective_id=0, has_side_effects=True, vmem_limit_bytes=48 * 1024 * 1024
        ),
    )(
        held(qkv), held(token_rate.reshape(1, tokens)), head_rate, held(fast_state[:, 0])
    )
    return combined, new_state[:, None]


def solution(mesh):
    count, heads = mesh.shape["seq"], mesh.shape["head"]
    plane = CORES
    while plane * plane < count:
        plane *= 2
    planes = count // plane

    def whole(qkv, token_rate, head_rate, fast_state):
        plane_tokens = token_rate.shape[0] // planes
        back = min(-(-(WINDOW - 1) // plane_tokens), planes - 1)
        return jax.shard_map(
            functools.partial(shards, (heads, planes, plane, back)),
            mesh=mesh,
            in_specs=(
                P(None, ("seq", "head"), None),
                P("seq", "head"),
                P("head"),
                P(None, "head", "seq", None),
            ),
            out_specs=(P(("seq", "head"), None), P(None, "head", "seq", None)),
            check_vma=False,
        )(qkv, token_rate, head_rate, fast_state)

    return whole
```

```python
import functools

import jax
import jax.numpy as jnp
from jax import lax
from jax.experimental import pallas as pl
from jax.experimental.pallas import tpu as pltpu
from jax.sharding import PartitionSpec as P

WINDOW = 1024
NS_STEPS = 2

ns_first = 3.4445
ns_second = -4.775
ns_third = 2.0315
rms_eps = 1e-06
norm_eps = 1e-07
lowest = -1e30

MESH = pl.DeviceIdType.MESH
CORES = 2
MATS = 3
SHARED = 2


def rms_scaled(values):
    return values * lax.rsqrt(jnp.mean(values * values, axis=-1, keepdims=True) + rms_eps)


def contract_last(left_side, right_side):
    return lax.dot_general(
        left_side, right_side, (((1,), (1,)), ((), ())), preferred_element_type=jnp.float32
    )


def low(values):
    return values.astype(jnp.bfloat16)


def dot(left_side, right_side):
    return jnp.dot(left_side, right_side, preferred_element_type=jnp.float32)


def kernel(
    sizes,
    qkv, rate, head_rate, state_hbm,
    out, new,
    state, step_smem, moved, new_rows, kv, q, q_from, o_send, o_from, l_send, l_from, w,
    gfull, gsend, grecv, g, wnew, direction, rates, comb, own_o, own_l,
    local_sem, q_sem, rate_sem, ky_sem, ks_sem, wz_sem, wy_sem, ws_sem,
    rs_sem, gz_sem, gy_sem, gs_sem, down_sem, up_sem, log_sem, o_sem, fresh_sem,
):
    heads, planes, plane, back = sizes
    rows_y = plane // CORES
    part = qkv.shape[1]
    tokens, width = q.shape
    hidden = direction.shape[1]
    state_rows = state.shape[1]
    link = w.dtype
    count = plane * tokens

    seq = lax.axis_index("seq")
    head = lax.axis_index("head")
    z = seq // plane
    p = lax.rem(seq, plane)
    y = p // CORES
    core = lax.rem(p, CORES)
    sibling = y * CORES + (1 - core)

    def device(z_at, p_at):
        return {"seq": z_at * plane + p_at, "head": head}

    def wrap(z_at):
        return lax.rem(z_at + 2 * planes, planes)

    def p_of_y(step, kind=0):
        return lax.rem(y + step, rows_y) * CORES + (1 - core if kind else core)

    def head_peer(step):
        return {"seq": seq, "head": lax.rem(head + step, heads)}

    def guarded(when, action):
        if when is None:
            action()
        else:
            pl.when(when)(action)

    def far_peer(turn, step):
        return {"seq": z * plane + p_of_y(turn), "head": lax.rem(head + step, heads)}

    far = [(turn, step) for turn in range(rows_y) for step in range(heads) if turn + step]
    peers = [far_peer(turn, step) for turn, step in far if step]
    peers += [device(z, lax.rem(p + step, plane)) for step in range(1, plane)]
    peers += [device(wrap(z + step), at) for step in range(1, planes) for at in (p, sibling)]
    barrier = pltpu.get_barrier_semaphore()
    for peer in peers:
        pl.semaphore_signal(barrier, inc=1, device_id=peer, device_id_type=MESH)

    def local(src, dst, index):
        copy = pltpu.make_async_copy(src, dst, local_sem.at[index])
        copy.start()
        return copy

    state_copy = local(state_hbm, state, 0)
    rate_copy = local(rate, rates.at[p], 1)
    step_copy = local(head_rate, step_smem, 2)

    started = []

    def send(src, dst, sem, place, target, when=None):
        copy = pltpu.make_async_remote_copy(
            src_ref=src,
            dst_ref=dst,
            send_sem=sem.at[(0,) + place],
            recv_sem=sem.at[(1,) + place],
            device_id=target,
            device_id_type=MESH,
        )
        guarded(when, copy.start)
        started.append((copy, when))
        return copy

    def arrived(ref, sem, place):
        pltpu.make_async_remote_copy(
            src_ref=ref,
            dst_ref=ref,
            send_sem=sem.at[(0,) + place],
            recv_sem=sem.at[(1,) + place],
            device_id=device(z, sibling),
            device_id_type=MESH,
        ).wait_recv()

    def part_rows(step):
        owner = lax.rem(head - step + heads, heads)
        return pl.ds(pl.multiple_of(owner * part, part), part)

    def head_columns(index):
        return pl.ds(pl.multiple_of(index * width, width), width)

    own_rows = part_rows(0)
    own_columns = head_columns(head)
    for level in range(1, back + 1):
        @pl.when(z < level)
        def _(level=level):
            o_from[level - 1] = jnp.zeros_like(o_from[level - 1])
            l_from[level - 1] = jnp.full_like(l_from[level - 1], lowest)
    pl.semaphore_wait(barrier, len(peers))

    k_copies = {}
    for turn, step in far[::-1]:
        k_copies[turn, step] = send(
            qkv.at[pl.ds(1, 2), :, head_columns(lax.rem(head + step, heads))],
            kv.at[0, :, p, own_rows],
            ky_sem, (turn, step), far_peer(turn, step),
        )
    own_kv = qkv.at[pl.ds(1, 2), :, own_columns]
    ks_copies = {
        (0, 0): send(own_kv, kv.at[0, :, p, own_rows], ks_sem, (0, 0), device(z, sibling))
    }
    q_copies = [
        send(
            qkv.at[0, :, head_columns(lax.rem(head + step, heads))],
            q.at[own_rows],
            q_sem, (step,), head_peer(step),
        )
        for step in range(1, heads)
    ]
    local_kv = local(own_kv, kv.at[0, :, p, own_rows], 3)
    local_q = local(qkv.at[0, :, own_columns], q.at[own_rows], 4)
    state_copy.wait()
    for mat in range(MATS):
        w[mat, z, p] = state[mat].astype(link)

    far_first = sorted(range(1, planes), key=lambda step: -min(step, planes - step))
    lower = 1 - z * 2 // planes
    near_first = [step + (planes - 2 * step) * lower for step in range(1, planes)]
    wz_copies = [
        send(w.at[:, z, p], w.at[:, z, p], wz_sem, (step,), device(wrap(z + step), p))
        for step in far_first
    ]
    rate_copy.wait()
    rate_copies = [
        send(rates.at[p], rates.at[p], rate_sem, (step,), device(z, lax.rem(p + step, plane)))
        for step in range(1, plane)
    ]
    for turn, step in far:
        k_copies[turn, step].wait_recv()
        block = kv.at[0, :, p_of_y(rows_y - turn), part_rows(step)]
        ks_copies[turn, step] = send(block, block, ks_sem, (turn, step), device(z, sibling))
    local_q.wait()
    for copy in q_copies:
        copy.wait_recv()

    downs = {}

    def descend(level):
        src = q if level == 1 else q_from.at[level - 2]
        when = (z >= 1) & (z + level - 1 < planes)
        downs[level] = send(
            src, q_from.at[level - 1], down_sem, (level,), device(wrap(z - 1), p), when
        )

    if back >= 1:
        descend(1)

    local_kv.wait()
    for copy in wz_copies + rate_copies:
        copy.wait_recv()
    for copy in ks_copies.values():
        copy.wait_recv()

    keys = kv[0, 0].reshape(count, width)
    values = kv[0, 1].reshape(count, width)
    key_norm = low(rms_scaled(keys.astype(jnp.float32)))
    rate_row = -jnp.concatenate([rates[index] for index in range(plane)], axis=1)
    column = [
        low(w[mat, :, p].reshape(planes * state_rows, width)) for mat in range(MATS)
    ]
    gate_act = contract_last(column[0], key_norm)
    up_act = contract_last(column[1], key_norm)
    back_grad = contract_last(column[2], values) * rate_row
    sigmoid_gate = jax.nn.sigmoid(gate_act)
    silu_gate = gate_act * sigmoid_gate
    lefts = (
        back_grad * up_act * sigmoid_gate * (1.0 + gate_act * (1.0 - sigmoid_gate)),
        back_grad * silu_gate,
        silu_gate * up_act * rate_row,
    )
    groups = (pl.ds(0, SHARED), pl.ds(SHARED, 1))
    rs_copies = {}
    for mat in range(MATS):
        total = dot(low(lefts[mat]), values if mat == SHARED else key_norm)
        total = total.reshape(planes, state_rows, width)
        gfull[mat] = total
        gsend[mat] = total.astype(link)
        if mat:
            group = mat - 1
            for step in far_first:
                rs_copies[group, step] = send(
                    gsend.at[groups[group], wrap(z + step)], grecv.at[groups[group], step - 1],
                    rs_sem, (group, step), device(wrap(z + step), p),
                )

    def attend(level):
        queries = q[...] if level == 0 else q_from[level - 1]
        scores = contract_last(queries, kv[0, 0].reshape(count, width)) * width ** (-0.5)
        query_pos = level * count + p * tokens + lax.broadcasted_iota(jnp.int32, scores.shape, 0)
        key_pos = lax.broadcasted_iota(jnp.int32, scores.shape, 1)
        visible = (key_pos <= query_pos) & (key_pos > query_pos - WINDOW)
        scores = jnp.where(visible, scores, -jnp.inf)
        row_max = jnp.maximum(jnp.max(scores, axis=1, keepdims=True), lowest)
        exp_scores = jnp.exp(scores - row_max)
        row_sum = jnp.sum(exp_scores, axis=1, keepdims=True)
        result = dot(low(exp_scores), kv[0, 1].reshape(count, width))
        result = result / jnp.maximum(row_sum, 1e-30)
        log_sum = jnp.where(row_sum > 0.0, row_max + jnp.log(jnp.maximum(row_sum, 1e-30)), lowest)
        if level == 0:
            own_o[...] = result
            own_l[...] = log_sum
        else:
            o_send[level - 1] = low(result)
            l_send[level - 1] = jnp.broadcast_to(log_sum, (tokens, tokens)).T[:1]

    def w_at(mat, p_at):
        return w.at[mat, :, p_at]

    w_copies = {}
    for turn in range(1, rows_y):
        for kind, mat in ((0, core), (1, 1 - core), (2, SHARED)):
            w_copies[kind, turn] = send(
                w_at(mat, p), w_at(mat, p), wy_sem, (kind, turn), device(z, p_of_y(turn, kind % 2))
            )
    for kind, mat in ((1, 1 - core), (2, SHARED)):
        w_copies[kind, 0] = send(
            w_at(mat, p), w_at(mat, p), ws_sem, (kind, 0), device(z, sibling)
        )
    attend(0)

    def attend_for(level):
        @pl.when(z + level < planes)
        def _():
            downs[level].wait_recv()
            attend(level)

    ups = {}

    def ascend(level):
        when = z + level < planes
        target = device(wrap(z + level), p)
        ups[level] = (
            send(o_send.at[level - 1], o_from.at[level - 1], up_sem, (level,), target, when),
            send(l_send.at[level - 1], l_from.at[level - 1], log_sem, (level,), target, when),
        )

    if back >= 1:
        attend_for(1)

    if back >= 2:
        descend(2)

    def rs_sum(group):
        places = groups[group]
        total = gfull[places, z]
        for step in near_first:
            arrived(gsend.at[places, z], rs_sem, (group, step))
        for step in range(1, planes):
            total = total + grecv[places, step - 1].astype(jnp.float32)
        g[places, z, p] = total.astype(link)

    def pass_on(piece, sem, place, target):
        return send(piece, piece, sem, place, target)

    rs_sum(0)
    for step in far_first:
        for kind, mat, at in ((0, core, p), (1, 1 - core, sibling)):
            pass_on(g.at[mat, z, p], gz_sem, (kind, step), device(wrap(z + step), at))
    for turn in range(1, rows_y):
        for kind, mat in ((0, core), (1, 1 - core)):
            pass_on(g.at[mat, z, p], gy_sem, (kind, turn, 0), device(z, p_of_y(turn, kind)))
    pass_on(g.at[1 - core, z, p], gs_sem, (1, 0, 0), device(z, sibling))

    def shared_on(step):
        piece = g.at[SHARED, wrap(z - step), p]
        for turn in range(1, rows_y):
            pass_on(piece, gy_sem, (2, turn, step), device(z, p_of_y(turn)))
        pass_on(piece, gs_sem, (2, 0, step), device(z, sibling))

    def shared_relay(step):
        for turn in range(1, rows_y):
            piece = g.at[SHARED, wrap(z - step), p_of_y(rows_y - turn)]
            arrived(piece, gy_sem, (2, turn, step))
            pass_on(piece, gs_sem, (2, turn, step), device(z, sibling))

    rs_sum(1)
    for step in far_first:
        pass_on(g.at[SHARED, z, p], gz_sem, (2, step), device(wrap(z + step), p))
    shared_on(0)
    if back >= 1:
        ascend(1)

    for step in near_first:
        for kind, at in ((0, p), (1, sibling)):
            piece = g.at[core, wrap(z - step), at]
            arrived(piece, gz_sem, (kind, step))
            for turn in range(1, rows_y):
                pass_on(piece, gy_sem, (kind, turn, step), device(z, p_of_y(turn)))
    for level in range(2, back + 1):
        attend_for(level)
        ascend(level)
        if level < back:
            descend(level + 1)
    for turn in range(1, rows_y):
        w_copies[2, turn].wait_recv()
        piece = w_at(SHARED, p_of_y(rows_y - turn))
        w_copies[3, turn] = send(piece, piece, ws_sem, (2, turn), device(z, sibling))
    query_norm = low(rms_scaled(q[...].astype(jnp.float32)))

    def shared_take(step):
        arrived(g.at[SHARED, wrap(z - step), p], gz_sem, (2, step))
        shared_on(step)

    for step in near_first[:-1]:
        shared_take(step)
    for key, copy in w_copies.items():
        if key not in [(2, turn) for turn in range(1, rows_y)]:
            copy.wait_recv()
    arrived(g.at[core, z, p], gs_sem, (1, 0, 0))
    for step in range(planes):
        for turn in range(1, rows_y):
            for kind in range(2):
                arrived(g.at[core, z, p], gy_sem, (kind, turn, step))

    step_copy.wait()
    step_size = step_smem[0]
    own = pl.ds(pl.multiple_of(seq * state_rows, state_rows), state_rows)

    def orthogonalize(mat, slot):
        full = g[mat].reshape(hidden, width)
        wide = full.astype(jnp.float32)
        scale = 1.0 / (jnp.sqrt(jnp.sum(wide * wide)) + norm_eps)
        gram = contract_last(low(full), low(full)) * (scale * scale)
        iterate = None
        for turn in range(NS_STEPS):
            if turn:
                yield
                gram = contract_last(low(iterate), low(iterate))
            gram_low = low(gram)
            poly = low(ns_second * gram + ns_third * dot(gram_low, gram_low))
            if turn:
                iterate = ns_first * iterate + dot(poly, low(iterate))
            else:
                iterate = scale * (ns_first * wide + dot(poly, low(full)))
        change = step_size * iterate
        direction[slot] = change
        wnew[mat] = low(w[mat].reshape(hidden, width).astype(jnp.float32) - change)
        new_rows[mat] = state[mat] - direction[slot, own, :]
        yield

    turns = orthogonalize(core, 0)
    next(turns)
    shared_take(near_first[-1])
    shared_relay(0)
    for step in near_first[:-1]:
        shared_relay(step)
    for _ in turns:
        pass
    sibling_seq = z * plane + sibling
    theirs = pl.ds(pl.multiple_of(sibling_seq * state_rows, state_rows), state_rows)
    swaps = [
        send(wnew.at[core], wnew.at[core], fresh_sem, (0,), device(z, sibling)),
        send(direction.at[0, theirs], moved, fresh_sem, (1,), device(z, sibling)),
    ]
    shared_relay(near_first[-1])
    for step in range(planes):
        for turn in range(rows_y):
            arrived(g.at[SHARED, z, p], gs_sem, (2, turn, step))
    for _ in orthogonalize(SHARED, 1):
        pass
    for level in range(1, back + 1):
        for copy in ups[level]:
            pl.when(z >= level)(copy.wait_recv)
    logs = [own_l[...]]
    for level in range(1, back + 1):
        row = jnp.broadcast_to(l_from[level - 1], (tokens, tokens))
        logs.append(row.T[:, :1])
    top = functools.reduce(jnp.maximum, logs)
    shares = [jnp.exp(log - top) for log in logs]
    attention = shares[0] * own_o[...]
    for level in range(1, back + 1):
        attention = attention + shares[level] * o_from[level - 1].astype(jnp.float32)
    attention = attention / functools.reduce(jnp.add, shares)
    for copy in swaps:
        copy.wait_recv()
    new_rows[1 - core] = state[1 - core] - moved[...]
    local_new = local(new_rows, new, 1)
    gate = contract_last(query_norm, wnew[0])
    active = low(gate * jax.nn.sigmoid(gate) * contract_last(query_norm, wnew[1]))
    comb[...] = low(attention + dot(active, wnew[SHARED]))

    o_copies = []
    for step in range(1, heads):
        target = lax.rem(head + step, heads)
        rows = pl.ds(pl.multiple_of(target * part, part), part)
        o_copies.append(
            send(comb.at[rows], out.at[:, own_columns], o_sem, (step,), head_peer(step))
        )
    local_out = local(comb.at[own_rows], out.at[:, own_columns], 0)
    local_out.wait()
    local_new.wait()
    for copy in o_copies:
        copy.wait_recv()
    for copy, when in started:
        guarded(when, copy.wait_send)


def hand_over(combined, new_state, combined_out, new_state_out, sems):
    first = pltpu.make_async_copy(combined, combined_out, sems.at[0])
    second = pltpu.make_async_copy(new_state, new_state_out, sems.at[1])
    first.start()
    second.start()
    first.wait()
    second.wait()


def held(values):
    return pltpu.with_memory_space_constraint(values, pltpu.HBM)


def shards(sizes, qkv, token_rate, head_rate, fast_state):
    heads, planes, plane, back = sizes
    part, width = qkv.shape[1], qkv.shape[2] // heads
    tokens = token_rate.shape[0]
    state_rows = fast_state.shape[2]
    hidden = state_rows * planes * plane
    rows_y = plane // CORES
    levels = max(back, 1)
    link = jnp.bfloat16 if state_rows % 16 == 0 else jnp.float32
    dma = pltpu.SemaphoreType.DMA
    hbm = pl.BlockSpec(memory_space=pltpu.HBM)
    combined, new_state = pl.pallas_call(
        functools.partial(kernel, sizes),
        name="block",
        out_shape=(
            jax.ShapeDtypeStruct((part, heads * width), jnp.bfloat16),
            jax.ShapeDtypeStruct((MATS, state_rows, width), jnp.float32),
        ),
        in_specs=[hbm] * 4,
        out_specs=(hbm, hbm),
        scratch_shapes=[
            pltpu.VMEM((MATS, state_rows, width), jnp.float32),
            pltpu.SMEM((1,), jnp.float32),
            pltpu.VMEM((state_rows, width), jnp.float32),
            pltpu.VMEM((MATS, state_rows, width), jnp.float32),
            pltpu.VMEM((1, 2, plane, tokens, width), jnp.bfloat16),
            pltpu.VMEM((tokens, width), jnp.bfloat16),
            pltpu.VMEM((levels, tokens, width), jnp.bfloat16),
            pltpu.VMEM((levels, tokens, width), jnp.bfloat16),
            pltpu.VMEM((levels, tokens, width), jnp.bfloat16),
            pltpu.VMEM((levels, 1, tokens), jnp.float32),
            pltpu.VMEM((levels, 1, tokens), jnp.float32),
            pltpu.VMEM((MATS, planes, plane, state_rows, width), link),
            pltpu.VMEM((MATS, planes, state_rows, width), jnp.float32),
            pltpu.VMEM((MATS, planes, state_rows, width), link),
            pltpu.VMEM((MATS, planes - 1, state_rows, width), link),
            pltpu.VMEM((MATS, planes, plane, state_rows, width), link),
            pltpu.VMEM((MATS, hidden, width), jnp.bfloat16),
            pltpu.VMEM((2, hidden, width), jnp.float32),
            pltpu.VMEM((plane, 1, tokens), jnp.float32),
            pltpu.VMEM((tokens, width), jnp.bfloat16),
            pltpu.VMEM((tokens, width), jnp.float32),
            pltpu.VMEM((tokens, 1), jnp.float32),
            dma((5,)),
            dma((2, heads)),
            dma((2, plane)),
            dma((2, rows_y, heads)),
            dma((2, rows_y, heads)),
            dma((2, planes)),
            dma((2, MATS, rows_y)),
            dma((2, MATS, rows_y)),
            dma((2, 2, planes)),
            dma((2, MATS, planes)),
            dma((2, MATS, rows_y, planes)),
            dma((2, MATS, rows_y, planes)),
            dma((2, back + 1)),
            dma((2, back + 1)),
            dma((2, back + 1)),
            dma((2, heads)),
            dma((2, 2)),
        ],
        compiler_params=pltpu.CompilerParams(
            collective_id=0, has_side_effects=True, vmem_limit_bytes=48 * 1024 * 1024
        ),
    )(
        held(qkv), held(token_rate.reshape(1, tokens)), head_rate, held(fast_state[:, 0])
    )
    return combined, new_state[:, None]


def solution(mesh):
    count, heads = mesh.shape["seq"], mesh.shape["head"]
    plane = CORES
    while plane * plane < count:
        plane *= 2
    planes = count // plane

    def whole(qkv, token_rate, head_rate, fast_state):
        plane_tokens = token_rate.shape[0] // planes
        back = min(-(-(WINDOW - 1) // plane_tokens), planes - 1)
        return jax.shard_map(
            functools.partial(shards, (heads, planes, plane, back)),
            mesh=mesh,
            in_specs=(
                P(None, ("seq", "head"), None),
                P("seq", "head"),
                P("head"),
                P(None, "head", "seq", None),
            ),
            out_specs=(P(("seq", "head"), None), P(None, "head", "seq", None)),
            check_vma=False,
        )(qkv, token_rate, head_rate, fast_state)

    return whole
```

```python
import functools

import jax
import jax.numpy as jnp
from jax import lax
from jax.experimental import pallas as pl
from jax.experimental.pallas import tpu as pltpu
from jax.sharding import PartitionSpec as P

WINDOW = 1024
NS_STEPS = 2

ns_first = 3.4445
ns_second = -4.775
ns_third = 2.0315
rms_eps = 1e-06
norm_eps = 1e-07
lowest = -1e30

MESH = pl.DeviceIdType.MESH
CORES = 2
MATS = 3
SHARED = 2


def rms_scaled(values):
    return values * lax.rsqrt(jnp.mean(values * values, axis=-1, keepdims=True) + rms_eps)


def contract_last(left_side, right_side):
    return lax.dot_general(
        left_side, right_side, (((1,), (1,)), ((), ())), preferred_element_type=jnp.float32
    )


def low(values):
    return values.astype(jnp.bfloat16)


def dot(left_side, right_side):
    return jnp.dot(left_side, right_side, preferred_element_type=jnp.float32)


def kernel(
    sizes,
    qkv, rate, head_rate, state_hbm,
    out, new,
    state, step_smem, moved, new_rows, kv, q, q_from, o_send, o_from, l_send, l_from, w,
    gfull, gsend, grecv, g, wnew, direction, rates, comb, own_o, own_l,
    local_sem, q_sem, rate_sem, ky_sem, ks_sem, wz_sem, wy_sem, ws_sem,
    rs_sem, gz_sem, gy_sem, gs_sem, down_sem, up_sem, log_sem, o_sem, fresh_sem,
):
    heads, planes, plane, back = sizes
    rows_y = plane // CORES
    part = qkv.shape[1]
    tokens, width = q.shape
    hidden = direction.shape[1]
    state_rows = state.shape[1]
    link = w.dtype
    count = plane * tokens

    seq = lax.axis_index("seq")
    head = lax.axis_index("head")
    z = seq // plane
    p = lax.rem(seq, plane)
    y = p // CORES
    core = lax.rem(p, CORES)
    sibling = y * CORES + (1 - core)

    def device(z_at, p_at):
        return {"seq": z_at * plane + p_at, "head": head}

    def wrap(z_at):
        return lax.rem(z_at + 2 * planes, planes)

    def p_of_y(step, kind=0):
        return lax.rem(y + step, rows_y) * CORES + (1 - core if kind else core)

    def head_peer(step):
        return {"seq": seq, "head": lax.rem(head + step, heads)}

    def guarded(when, action):
        if when is None:
            action()
        else:
            pl.when(when)(action)

    def far_peer(turn, step):
        return {"seq": z * plane + p_of_y(turn), "head": lax.rem(head + step, heads)}

    far = [(turn, step) for turn in range(rows_y) for step in range(heads) if turn + step]
    peers = [far_peer(turn, step) for turn, step in far if step]
    peers += [device(z, lax.rem(p + step, plane)) for step in range(1, plane)]
    peers += [device(wrap(z + step), at) for step in range(1, planes) for at in (p, sibling)]
    barrier = pltpu.get_barrier_semaphore()
    for peer in peers:
        pl.semaphore_signal(barrier, inc=1, device_id=peer, device_id_type=MESH)

    def local(src, dst, index):
        copy = pltpu.make_async_copy(src, dst, local_sem.at[index])
        copy.start()
        return copy

    state_copy = local(state_hbm, state, 0)
    rate_copy = local(rate, rates.at[p], 1)
    step_copy = local(head_rate, step_smem, 2)

    started = []

    def send(src, dst, sem, place, target, when=None):
        copy = pltpu.make_async_remote_copy(
            src_ref=src,
            dst_ref=dst,
            send_sem=sem.at[(0,) + place],
            recv_sem=sem.at[(1,) + place],
            device_id=target,
            device_id_type=MESH,
        )
        guarded(when, copy.start)
        started.append((copy, when))
        return copy

    def arrived(ref, sem, place):
        pltpu.make_async_remote_copy(
            src_ref=ref,
            dst_ref=ref,
            send_sem=sem.at[(0,) + place],
            recv_sem=sem.at[(1,) + place],
            device_id=device(z, sibling),
            device_id_type=MESH,
        ).wait_recv()

    def part_rows(step):
        owner = lax.rem(head - step + heads, heads)
        return pl.ds(pl.multiple_of(owner * part, part), part)

    def head_columns(index):
        return pl.ds(pl.multiple_of(index * width, width), width)

    own_rows = part_rows(0)
    own_columns = head_columns(head)
    for level in range(1, back + 1):
        @pl.when(z < level)
        def _(level=level):
            o_from[level - 1] = jnp.zeros_like(o_from[level - 1])
            l_from[level - 1] = jnp.full_like(l_from[level - 1], lowest)
    pl.semaphore_wait(barrier, len(peers))

    q_copies = [
        send(
            qkv.at[0, :, head_columns(lax.rem(head + step, heads))],
            q.at[own_rows],
            q_sem, (step,), head_peer(step),
        )
        for step in range(1, heads)
    ]
    local_q = local(qkv.at[0, :, own_columns], q.at[own_rows], 4)
    k_copies = {}
    for turn, step in far[::-1]:
        k_copies[turn, step] = send(
            qkv.at[pl.ds(1, 2), :, head_columns(lax.rem(head + step, heads))],
            kv.at[0, :, p, own_rows],
            ky_sem, (turn, step), far_peer(turn, step),
        )
    own_kv = qkv.at[pl.ds(1, 2), :, own_columns]
    ks_copies = {
        (0, 0): send(own_kv, kv.at[0, :, p, own_rows], ks_sem, (0, 0), device(z, sibling))
    }
    local_kv = local(own_kv, kv.at[0, :, p, own_rows], 3)
    state_copy.wait()
    for mat in range(MATS):
        w[mat, z, p] = state[mat].astype(link)

    lower = 1 - z * 2 // planes
    near_first = [step + (planes - 2 * step) * lower for step in range(1, planes)]
    wz_copies = [
        send(w.at[:, z, p], w.at[:, z, p], wz_sem, (step,), device(wrap(z + step), p))
        for step in near_first
    ]
    rate_copy.wait()
    rate_copies = [
        send(rates.at[p], rates.at[p], rate_sem, (step,), device(z, lax.rem(p + step, plane)))
        for step in range(1, plane)
    ]
    local_q.wait()
    for copy in q_copies:
        copy.wait_recv()

    downs = {}

    def descend(level):
        src = q if level == 1 else q_from.at[level - 2]
        when = (z >= 1) & (z + level - 1 < planes)
        downs[level] = send(
            src, q_from.at[level - 1], down_sem, (level,), device(wrap(z - 1), p), when
        )

    if back >= 1:
        descend(1)

    for turn, step in far:
        k_copies[turn, step].wait_recv()
        block = kv.at[0, :, p_of_y(rows_y - turn), part_rows(step)]
        ks_copies[turn, step] = send(block, block, ks_sem, (turn, step), device(z, sibling))
    local_kv.wait()
    for copy in wz_copies + rate_copies:
        copy.wait_recv()
    for copy in ks_copies.values():
        copy.wait_recv()

    keys = kv[0, 0].reshape(count, width)
    values = kv[0, 1].reshape(count, width)
    key_norm = low(rms_scaled(keys.astype(jnp.float32)))
    rate_row = -jnp.concatenate([rates[index] for index in range(plane)], axis=1)
    column = [
        low(w[mat, :, p].reshape(planes * state_rows, width)) for mat in range(MATS)
    ]
    gate_act = contract_last(column[0], key_norm)
    up_act = contract_last(column[1], key_norm)
    back_grad = contract_last(column[2], values) * rate_row
    sigmoid_gate = jax.nn.sigmoid(gate_act)
    silu_gate = gate_act * sigmoid_gate
    lefts = (
        back_grad * up_act * sigmoid_gate * (1.0 + gate_act * (1.0 - sigmoid_gate)),
        back_grad * silu_gate,
        silu_gate * up_act * rate_row,
    )
    groups = (pl.ds(0, SHARED), pl.ds(SHARED, 1))
    for mat in range(MATS):
        total = dot(low(lefts[mat]), values if mat == SHARED else key_norm)
        total = total.reshape(planes, state_rows, width)
        gfull[mat] = total
        gsend[mat] = total.astype(link)
        if mat:
            group = mat - 1
            for step in near_first:
                send(
                    gsend.at[groups[group], wrap(z + step)], grecv.at[groups[group], step - 1],
                    rs_sem, (group, step), device(wrap(z + step), p),
                )

    def attend(level):
        queries = q[...] if level == 0 else q_from[level - 1]
        scores = contract_last(queries, kv[0, 0].reshape(count, width)) * width ** (-0.5)
        query_pos = level * count + p * tokens + lax.broadcasted_iota(jnp.int32, scores.shape, 0)
        key_pos = lax.broadcasted_iota(jnp.int32, scores.shape, 1)
        visible = (key_pos <= query_pos) & (key_pos > query_pos - WINDOW)
        scores = jnp.where(visible, scores, -jnp.inf)
        row_max = jnp.maximum(jnp.max(scores, axis=1, keepdims=True), lowest)
        exp_scores = jnp.exp(scores - row_max)
        row_sum = jnp.sum(exp_scores, axis=1, keepdims=True)
        result = dot(low(exp_scores), kv[0, 1].reshape(count, width))
        result = result / jnp.maximum(row_sum, 1e-30)
        log_sum = jnp.where(row_sum > 0.0, row_max + jnp.log(jnp.maximum(row_sum, 1e-30)), lowest)
        if level == 0:
            own_o[...] = result
            own_l[...] = log_sum
        else:
            o_send[level - 1] = low(result)
            l_send[level - 1] = jnp.broadcast_to(log_sum, (tokens, tokens)).T[:1]

    def w_at(mat, p_at):
        return w.at[mat, :, p_at]

    w_copies = {}
    for turn in range(1, rows_y):
        for kind, mat in ((0, core), (1, 1 - core), (2, SHARED)):
            w_copies[kind, turn] = send(
                w_at(mat, p), w_at(mat, p), wy_sem, (kind, turn), device(z, p_of_y(turn, kind % 2))
            )
    for kind, mat in ((1, 1 - core), (2, SHARED)):
        w_copies[kind, 0] = send(
            w_at(mat, p), w_at(mat, p), ws_sem, (kind, 0), device(z, sibling)
        )
    attend(0)

    def attend_for(level):
        @pl.when(z + level < planes)
        def _():
            if level > 1:
                downs[level].wait_recv()
            attend(level)

    ups = {}

    def ascend(level):
        when = z + level < planes
        target = device(wrap(z + level), p)
        ups[level] = (
            send(o_send.at[level - 1], o_from.at[level - 1], up_sem, (level,), target, when),
            send(l_send.at[level - 1], l_from.at[level - 1], log_sem, (level,), target, when),
        )

    if back >= 1:
        pl.when(z + 1 < planes)(downs[1].wait_recv)
    if back >= 1:
        attend_for(1)

    def drain():
        for copy, when in started:
            guarded(when, copy.wait_send)
        started.clear()

    def rs_sum(group):
        places = groups[group]
        total = gfull[places, z]
        for step in near_first:
            arrived(gsend.at[places, z], rs_sem, (group, step))
        for step in range(1, planes):
            total = total + grecv[places, step - 1].astype(jnp.float32)
        g[places, z, p] = total.astype(link)

    def pass_on(piece, sem, place, target):
        return send(piece, piece, sem, place, target)

    rs_sum(0)
    for step in near_first:
        for kind, mat, at in ((0, core, p), (1, 1 - core, sibling)):
            pass_on(g.at[mat, z, p], gz_sem, (kind, step), device(wrap(z + step), at))
    for turn in range(1, rows_y):
        for kind, mat in ((0, core), (1, 1 - core)):
            pass_on(g.at[mat, z, p], gy_sem, (kind, turn, 0), device(z, p_of_y(turn, kind)))
    pass_on(g.at[1 - core, z, p], gs_sem, (1, 0, 0), device(z, sibling))

    def shared_on(step):
        piece = g.at[SHARED, wrap(z - step), p]
        for turn in range(1, rows_y):
            for kind in range(2):
                target = device(z, p_of_y(turn, kind))
                pass_on(piece, gy_sem, (SHARED + kind, turn, step), target)
        pass_on(piece, gs_sem, (2, 0, step), device(z, sibling))

    if back >= 2:
        descend(2)
    rs_sum(1)
    for step in near_first:
        pass_on(g.at[SHARED, z, p], gz_sem, (2, step), device(wrap(z + step), p))
    shared_on(0)
    if back >= 1:
        ascend(1)

    for step in near_first:
        for kind, at in ((0, p), (1, sibling)):
            piece = g.at[core, wrap(z - step), at]
            arrived(piece, gz_sem, (kind, step))
            for turn in range(1, rows_y):
                pass_on(piece, gy_sem, (kind, turn, step), device(z, p_of_y(turn)))
    for level in range(2, back + 1):
        attend_for(level)
        ascend(level)
        if level < back:
            descend(level + 1)
    for turn in range(1, rows_y):
        w_copies[2, turn].wait_recv()
        piece = w_at(SHARED, p_of_y(rows_y - turn))
        w_copies[3, turn] = send(piece, piece, ws_sem, (2, turn), device(z, sibling))
    query_norm = low(rms_scaled(q[...].astype(jnp.float32)))

    def shared_take(step):
        arrived(g.at[SHARED, wrap(z - step), p], gz_sem, (2, step))
        shared_on(step)

    for step in near_first:
        shared_take(step)
    for key, copy in w_copies.items():
        if key not in [(2, turn) for turn in range(1, rows_y)]:
            copy.wait_recv()
    arrived(g.at[core, z, p], gs_sem, (1, 0, 0))
    for step in range(planes):
        for turn in range(1, rows_y):
            for kind in range(2):
                arrived(g.at[core, z, p], gy_sem, (kind, turn, step))

    step_copy.wait()
    step_size = step_smem[0]
    own = pl.ds(pl.multiple_of(seq * state_rows, state_rows), state_rows)

    def orthogonalize(mat, slot):
        full = g[mat].reshape(hidden, width)
        wide = full.astype(jnp.float32)
        scale = 1.0 / (jnp.sqrt(jnp.sum(wide * wide)) + norm_eps)
        gram = contract_last(low(full), low(full)) * (scale * scale)
        iterate = None
        for turn in range(NS_STEPS):
            if turn:
                gram = contract_last(low(iterate), low(iterate))
            gram_low = low(gram)
            poly = low(ns_second * gram + ns_third * dot(gram_low, gram_low))
            if turn:
                iterate = ns_first * iterate + dot(poly, low(iterate))
            else:
                iterate = scale * (ns_first * wide + dot(poly, low(full)))
        change = step_size * iterate
        direction[slot] = change
        wnew[mat] = low(w[mat].reshape(hidden, width).astype(jnp.float32) - change)
        new_rows[mat] = state[mat] - direction[slot, own, :]

    orthogonalize(core, 0)
    sibling_seq = z * plane + sibling
    theirs = pl.ds(pl.multiple_of(sibling_seq * state_rows, state_rows), state_rows)
    swaps = [
        send(wnew.at[core], wnew.at[core], fresh_sem, (0,), device(z, sibling)),
        send(direction.at[0, theirs], moved, fresh_sem, (1,), device(z, sibling)),
    ]
    for step in range(planes):
        arrived(g.at[SHARED, z, p], gs_sem, (2, 0, step))
        for turn in range(1, rows_y):
            for kind in range(2):
                arrived(g.at[SHARED, z, p], gy_sem, (SHARED + kind, turn, step))
    orthogonalize(SHARED, 1)
    for level in range(1, back + 1):
        for copy in ups[level]:
            pl.when(z >= level)(copy.wait_recv)
    logs = [own_l[...]]
    for level in range(1, back + 1):
        row = jnp.broadcast_to(l_from[level - 1], (tokens, tokens))
        logs.append(row.T[:, :1])
    top = functools.reduce(jnp.maximum, logs)
    shares = [jnp.exp(log - top) for log in logs]
    attention = shares[0] * own_o[...]
    for level in range(1, back + 1):
        attention = attention + shares[level] * o_from[level - 1].astype(jnp.float32)
    attention = attention / functools.reduce(jnp.add, shares)
    for copy in swaps:
        copy.wait_recv()
    new_rows[1 - core] = state[1 - core] - moved[...]
    local_new = local(new_rows, new, 1)
    gate = contract_last(query_norm, wnew[0])
    active = low(gate * jax.nn.sigmoid(gate) * contract_last(query_norm, wnew[1]))
    comb[...] = low(attention + dot(active, wnew[SHARED]))

    o_copies = []
    for step in range(1, heads):
        target = lax.rem(head + step, heads)
        rows = pl.ds(pl.multiple_of(target * part, part), part)
        o_copies.append(
            send(comb.at[rows], out.at[:, own_columns], o_sem, (step,), head_peer(step))
        )
    local_out = local(comb.at[own_rows], out.at[:, own_columns], 0)
    local_out.wait()
    local_new.wait()
    for copy in o_copies:
        copy.wait_recv()
    drain()


def hand_over(combined, new_state, combined_out, new_state_out, sems):
    first = pltpu.make_async_copy(combined, combined_out, sems.at[0])
    second = pltpu.make_async_copy(new_state, new_state_out, sems.at[1])
    first.start()
    second.start()
    first.wait()
    second.wait()


def held(values):
    return pltpu.with_memory_space_constraint(values, pltpu.HBM)


def shards(sizes, qkv, token_rate, head_rate, fast_state):
    heads, planes, plane, back = sizes
    part, width = qkv.shape[1], qkv.shape[2] // heads
    tokens = token_rate.shape[0]
    state_rows = fast_state.shape[2]
    hidden = state_rows * planes * plane
    rows_y = plane // CORES
    levels = max(back, 1)
    link = jnp.bfloat16 if state_rows % 16 == 0 else jnp.float32
    dma = pltpu.SemaphoreType.DMA
    hbm = pl.BlockSpec(memory_space=pltpu.HBM)
    combined, new_state = pl.pallas_call(
        functools.partial(kernel, sizes),
        name="block",
        out_shape=(
            jax.ShapeDtypeStruct((part, heads * width), jnp.bfloat16),
            jax.ShapeDtypeStruct((MATS, state_rows, width), jnp.float32),
        ),
        in_specs=[hbm] * 4,
        out_specs=(hbm, hbm),
        scratch_shapes=[
            pltpu.VMEM((MATS, state_rows, width), jnp.float32),
            pltpu.SMEM((1,), jnp.float32),
            pltpu.VMEM((state_rows, width), jnp.float32),
            pltpu.VMEM((MATS, state_rows, width), jnp.float32),
            pltpu.VMEM((1, 2, plane, tokens, width), jnp.bfloat16),
            pltpu.VMEM((tokens, width), jnp.bfloat16),
            pltpu.VMEM((levels, tokens, width), jnp.bfloat16),
            pltpu.VMEM((levels, tokens, width), jnp.bfloat16),
            pltpu.VMEM((levels, tokens, width), jnp.bfloat16),
            pltpu.VMEM((levels, 1, tokens), jnp.float32),
            pltpu.VMEM((levels, 1, tokens), jnp.float32),
            pltpu.VMEM((MATS, planes, plane, state_rows, width), link),
            pltpu.VMEM((MATS, planes, state_rows, width), jnp.float32),
            pltpu.VMEM((MATS, planes, state_rows, width), link),
            pltpu.VMEM((MATS, planes - 1, state_rows, width), link),
            pltpu.VMEM((MATS, planes, plane, state_rows, width), link),
            pltpu.VMEM((MATS, hidden, width), jnp.bfloat16),
            pltpu.VMEM((2, hidden, width), jnp.float32),
            pltpu.VMEM((plane, 1, tokens), jnp.float32),
            pltpu.VMEM((tokens, width), jnp.bfloat16),
            pltpu.VMEM((tokens, width), jnp.float32),
            pltpu.VMEM((tokens, 1), jnp.float32),
            dma((5,)),
            dma((2, heads)),
            dma((2, plane)),
            dma((2, rows_y, heads)),
            dma((2, rows_y, heads)),
            dma((2, planes)),
            dma((2, MATS, rows_y)),
            dma((2, MATS, rows_y)),
            dma((2, 2, planes)),
            dma((2, MATS, planes)),
            dma((2, MATS + 1, rows_y, planes)),
            dma((2, MATS, rows_y, planes)),
            dma((2, back + 1)),
            dma((2, back + 1)),
            dma((2, back + 1)),
            dma((2, heads)),
            dma((2, 2)),
        ],
        compiler_params=pltpu.CompilerParams(
            collective_id=0, has_side_effects=True, vmem_limit_bytes=48 * 1024 * 1024
        ),
    )(
        held(qkv), held(token_rate.reshape(1, tokens)), head_rate, held(fast_state[:, 0])
    )
    return combined, new_state[:, None]


def solution(mesh):
    count, heads = mesh.shape["seq"], mesh.shape["head"]
    plane = CORES
    while plane * plane < count:
        plane *= 2
    planes = count // plane

    def whole(qkv, token_rate, head_rate, fast_state):
        plane_tokens = token_rate.shape[0] // planes
        back = min(-(-(WINDOW - 1) // plane_tokens), planes - 1)
        return jax.shard_map(
            functools.partial(shards, (heads, planes, plane, back)),
            mesh=mesh,
            in_specs=(
                P(None, ("seq", "head"), None),
                P("seq", "head"),
                P("head"),
                P(None, "head", "seq", None),
            ),
            out_specs=(P(("seq", "head"), None), P(None, "head", "seq", None)),
            check_vma=False,
        )(qkv, token_rate, head_rate, fast_state)

    return whole
```

```python
import functools

import jax
import jax.numpy as jnp
from jax import lax
from jax.experimental import pallas as pl
from jax.experimental.pallas import tpu as pltpu
from jax.sharding import PartitionSpec as P

WINDOW = 1024
NS_STEPS = 2

ns_first = 3.4445
ns_second = -4.775
ns_third = 2.0315
rms_eps = 1e-06
norm_eps = 1e-07
lowest = -1e30

MESH = pl.DeviceIdType.MESH
CORES = 2
MATS = 3
SHARED = 2


def rms_scaled(values):
    return values * lax.rsqrt(jnp.mean(values * values, axis=-1, keepdims=True) + rms_eps)


def contract_last(left_side, right_side):
    return lax.dot_general(
        left_side, right_side, (((1,), (1,)), ((), ())), preferred_element_type=jnp.float32
    )


def low(values):
    return values.astype(jnp.bfloat16)


def dot(left_side, right_side):
    return jnp.dot(left_side, right_side, preferred_element_type=jnp.float32)


def kernel(
    sizes,
    qkv, rate, head_rate, state_hbm,
    out, new,
    state, step_smem, moved, new_rows, kv, q, q_from, o_send, o_from, l_send, l_from, w,
    gfull, gsend, grecv, g, wnew, direction, rates, comb, own_o, own_l,
    local_sem, q_sem, rate_sem, ky_sem, ks_sem, wz_sem, wy_sem, ws_sem,
    rs_sem, gz_sem, gy_sem, gs_sem, down_sem, up_sem, log_sem, o_sem, fresh_sem,
):
    heads, planes, plane, back = sizes
    rows_y = plane // CORES
    part = qkv.shape[1]
    tokens, width = q.shape
    hidden = direction.shape[1]
    state_rows = state.shape[1]
    link = w.dtype
    count = plane * tokens

    seq = lax.axis_index("seq")
    head = lax.axis_index("head")
    z = seq // plane
    p = lax.rem(seq, plane)
    y = p // CORES
    core = lax.rem(p, CORES)
    sibling = y * CORES + (1 - core)

    def device(z_at, p_at):
        return {"seq": z_at * plane + p_at, "head": head}

    def wrap(z_at):
        return lax.rem(z_at + 2 * planes, planes)

    def p_of_y(step, kind=0):
        return lax.rem(y + step, rows_y) * CORES + (1 - core if kind else core)

    def head_peer(step):
        return {"seq": seq, "head": lax.rem(head + step, heads)}

    def guarded(when, action):
        if when is None:
            action()
        else:
            pl.when(when)(action)

    def far_peer(turn, step):
        return {"seq": z * plane + p_of_y(turn), "head": lax.rem(head + step, heads)}

    far = [(turn, step) for turn in range(rows_y) for step in range(heads) if turn + step]
    peers = [far_peer(turn, step) for turn, step in far if step]
    peers += [device(z, lax.rem(p + step, plane)) for step in range(1, plane)]
    peers += [device(wrap(z + step), at) for step in range(1, planes) for at in (p, sibling)]
    barrier = pltpu.get_barrier_semaphore()
    for peer in peers:
        pl.semaphore_signal(barrier, inc=1, device_id=peer, device_id_type=MESH)

    def local(src, dst, index):
        copy = pltpu.make_async_copy(src, dst, local_sem.at[index])
        copy.start()
        return copy

    state_copy = local(state_hbm, state, 0)
    rate_copy = local(rate, rates.at[p], 1)
    step_copy = local(head_rate, step_smem, 2)

    started = []

    def send(src, dst, sem, place, target, when=None):
        copy = pltpu.make_async_remote_copy(
            src_ref=src,
            dst_ref=dst,
            send_sem=sem.at[(0,) + place],
            recv_sem=sem.at[(1,) + place],
            device_id=target,
            device_id_type=MESH,
        )
        guarded(when, copy.start)
        started.append((copy, when))
        return copy

    def arrived(ref, sem, place):
        pltpu.make_async_remote_copy(
            src_ref=ref,
            dst_ref=ref,
            send_sem=sem.at[(0,) + place],
            recv_sem=sem.at[(1,) + place],
            device_id=device(z, sibling),
            device_id_type=MESH,
        ).wait_recv()

    def part_rows(step):
        owner = lax.rem(head - step + heads, heads)
        return pl.ds(pl.multiple_of(owner * part, part), part)

    def head_columns(index):
        return pl.ds(pl.multiple_of(index * width, width), width)

    own_rows = part_rows(0)
    own_columns = head_columns(head)
    for level in range(1, back + 1):
        @pl.when(z < level)
        def _(level=level):
            o_from[level - 1] = jnp.zeros_like(o_from[level - 1])
            l_from[level - 1] = jnp.full_like(l_from[level - 1], lowest)
    state_copy.wait()
    for mat in range(MATS):
        w[mat, z, p] = state[mat].astype(link)
    pl.semaphore_wait(barrier, len(peers))

    lower = 1 - z * 2 // planes
    near_first = [step + (planes - 2 * step) * lower for step in range(1, planes)]
    wz_copies = [
        send(w.at[:, z, p], w.at[:, z, p], wz_sem, (step,), device(wrap(z + step), p))
        for step in near_first
    ]

    local_q = local(qkv.at[0, :, own_columns], q.at[own_rows], 4)
    k_copies = {}
    for turn, step in far[::-1]:
        k_copies[turn, step] = send(
            qkv.at[pl.ds(1, 2), :, head_columns(lax.rem(head + step, heads))],
            kv.at[0, :, p, own_rows],
            ky_sem, (turn, step), far_peer(turn, step),
        )
    q_copies = [
        send(
            qkv.at[0, :, head_columns(lax.rem(head + step, heads))],
            q.at[own_rows],
            q_sem, (step,), head_peer(step),
        )
        for step in range(1, heads)
    ]
    own_kv = qkv.at[pl.ds(1, 2), :, own_columns]
    ks_copies = {
        (0, 0): send(own_kv, kv.at[0, :, p, own_rows], ks_sem, (0, 0), device(z, sibling))
    }
    local_kv = local(own_kv, kv.at[0, :, p, own_rows], 3)
    rate_copy.wait()
    rate_copies = [
        send(rates.at[p], rates.at[p], rate_sem, (step,), device(z, lax.rem(p + step, plane)))
        for step in range(1, plane)
    ]
    for turn, step in far:
        k_copies[turn, step].wait_recv()
        block = kv.at[0, :, p_of_y(rows_y - turn), part_rows(step)]
        ks_copies[turn, step] = send(block, block, ks_sem, (turn, step), device(z, sibling))
    local_q.wait()
    for copy in q_copies:
        copy.wait_recv()

    downs = {}

    def descend(level):
        src = q if level == 1 else q_from.at[level - 2]
        when = (z >= 1) & (z + level - 1 < planes)
        downs[level] = send(
            src, q_from.at[level - 1], down_sem, (level,), device(wrap(z - 1), p), when
        )

    if back >= 1:
        descend(1)
    local_kv.wait()
    for copy in wz_copies + rate_copies:
        copy.wait_recv()
    for copy in ks_copies.values():
        copy.wait_recv()

    keys = kv[0, 0].reshape(count, width)
    values = kv[0, 1].reshape(count, width)
    key_norm = low(rms_scaled(keys.astype(jnp.float32)))
    rate_row = -jnp.concatenate([rates[index] for index in range(plane)], axis=1)
    column = [
        low(w[mat, :, p].reshape(planes * state_rows, width)) for mat in range(MATS)
    ]
    gate_act = contract_last(column[0], key_norm)
    up_act = contract_last(column[1], key_norm)
    back_grad = contract_last(column[2], values) * rate_row
    sigmoid_gate = jax.nn.sigmoid(gate_act)
    silu_gate = gate_act * sigmoid_gate
    lefts = (
        back_grad * up_act * sigmoid_gate * (1.0 + gate_act * (1.0 - sigmoid_gate)),
        back_grad * silu_gate,
        silu_gate * up_act * rate_row,
    )
    groups = (pl.ds(0, SHARED), pl.ds(SHARED, 1))
    for mat in range(MATS):
        total = dot(low(lefts[mat]), values if mat == SHARED else key_norm)
        total = total.reshape(planes, state_rows, width)
        gfull[mat] = total
        gsend[mat] = total.astype(link)
        if mat:
            group = mat - 1
            for step in near_first:
                send(
                    gsend.at[groups[group], wrap(z + step)], grecv.at[groups[group], step - 1],
                    rs_sem, (group, step), device(wrap(z + step), p),
                )

    def attend(level):
        queries = q[...] if level == 0 else q_from[level - 1]
        scores = contract_last(queries, kv[0, 0].reshape(count, width)) * width ** (-0.5)
        query_pos = level * count + p * tokens + lax.broadcasted_iota(jnp.int32, scores.shape, 0)
        key_pos = lax.broadcasted_iota(jnp.int32, scores.shape, 1)
        visible = (key_pos <= query_pos) & (key_pos > query_pos - WINDOW)
        scores = jnp.where(visible, scores, -jnp.inf)
        row_max = jnp.maximum(jnp.max(scores, axis=1, keepdims=True), lowest)
        exp_scores = jnp.exp(scores - row_max)
        row_sum = jnp.sum(exp_scores, axis=1, keepdims=True)
        result = dot(low(exp_scores), kv[0, 1].reshape(count, width))
        result = result / jnp.maximum(row_sum, 1e-30)
        log_sum = jnp.where(row_sum > 0.0, row_max + jnp.log(jnp.maximum(row_sum, 1e-30)), lowest)
        if level == 0:
            own_o[...] = result
            own_l[...] = log_sum
        else:
            o_send[level - 1] = low(result)
            l_send[level - 1] = jnp.broadcast_to(log_sum, (tokens, tokens)).T[:1]

    def w_at(mat, p_at):
        return w.at[mat, :, p_at]

    w_copies = {}
    for turn in range(1, rows_y):
        for kind, mat in ((0, core), (1, 1 - core), (2, SHARED)):
            w_copies[kind, turn] = send(
                w_at(mat, p), w_at(mat, p), wy_sem, (kind, turn), device(z, p_of_y(turn, kind % 2))
            )
    for kind, mat in ((1, 1 - core), (2, SHARED)):
        w_copies[kind, 0] = send(
            w_at(mat, p), w_at(mat, p), ws_sem, (kind, 0), device(z, sibling)
        )
    attend(0)

    def attend_for(level):
        @pl.when(z + level < planes)
        def _():
            if level > 1:
                downs[level].wait_recv()
            attend(level)

    ups = {}

    def ascend(level):
        when = z + level < planes
        target = device(wrap(z + level), p)
        ups[level] = (
            send(o_send.at[level - 1], o_from.at[level - 1], up_sem, (level,), target, when),
            send(l_send.at[level - 1], l_from.at[level - 1], log_sem, (level,), target, when),
        )

    if back >= 1:
        pl.when(z + 1 < planes)(downs[1].wait_recv)
    if back >= 1:
        attend_for(1)

    def drain():
        for copy, when in started:
            guarded(when, copy.wait_send)
        started.clear()

    def rs_sum(group):
        places = groups[group]
        total = gfull[places, z]
        for step in near_first:
            arrived(gsend.at[places, z], rs_sem, (group, step))
        for step in range(1, planes):
            total = total + grecv[places, step - 1].astype(jnp.float32)
        g[places, z, p] = total.astype(link)

    def pass_on(piece, sem, place, target):
        return send(piece, piece, sem, place, target)

    rs_sum(0)
    for step in near_first:
        for kind, mat, at in ((0, core, p), (1, 1 - core, sibling)):
            pass_on(g.at[mat, z, p], gz_sem, (kind, step), device(wrap(z + step), at))
    for turn in range(1, rows_y):
        for kind, mat in ((0, core), (1, 1 - core)):
            pass_on(g.at[mat, z, p], gy_sem, (kind, turn, 0), device(z, p_of_y(turn, kind)))
    pass_on(g.at[1 - core, z, p], gs_sem, (1, 0, 0), device(z, sibling))

    def shared_on(step):
        piece = g.at[SHARED, wrap(z - step), p]
        for turn in range(1, rows_y):
            for kind in range(2):
                target = device(z, p_of_y(turn, kind))
                pass_on(piece, gy_sem, (SHARED + kind, turn, step), target)
        pass_on(piece, gs_sem, (2, 0, step), device(z, sibling))

    if back >= 2:
        descend(2)
    rs_sum(1)
    for step in near_first:
        pass_on(g.at[SHARED, z, p], gz_sem, (2, step), device(wrap(z + step), p))
    shared_on(0)
    if back >= 1:
        ascend(1)

    for step in near_first:
        for kind, at in ((0, p), (1, sibling)):
            piece = g.at[core, wrap(z - step), at]
            arrived(piece, gz_sem, (kind, step))
            for turn in range(1, rows_y):
                pass_on(piece, gy_sem, (kind, turn, step), device(z, p_of_y(turn)))
    for level in range(2, back + 1):
        attend_for(level)
        ascend(level)
        if level < back:
            descend(level + 1)
    for turn in range(1, rows_y):
        w_copies[2, turn].wait_recv()
        piece = w_at(SHARED, p_of_y(rows_y - turn))
        w_copies[3, turn] = send(piece, piece, ws_sem, (2, turn), device(z, sibling))
    query_norm = low(rms_scaled(q[...].astype(jnp.float32)))

    def shared_take(step):
        arrived(g.at[SHARED, wrap(z - step), p], gz_sem, (2, step))
        shared_on(step)

    for step in near_first:
        shared_take(step)
    for key, copy in w_copies.items():
        if key not in [(2, turn) for turn in range(1, rows_y)]:
            copy.wait_recv()
    arrived(g.at[core, z, p], gs_sem, (1, 0, 0))
    for step in range(planes):
        for turn in range(1, rows_y):
            for kind in range(2):
                arrived(g.at[core, z, p], gy_sem, (kind, turn, step))

    step_copy.wait()
    step_size = step_smem[0]
    own = pl.ds(pl.multiple_of(seq * state_rows, state_rows), state_rows)

    def orthogonalize(mat, slot):
        full = g[mat].reshape(hidden, width)
        wide = full.astype(jnp.float32)
        scale = 1.0 / (jnp.sqrt(jnp.sum(wide * wide)) + norm_eps)
        gram = contract_last(low(full), low(full)) * (scale * scale)
        iterate = None
        for turn in range(NS_STEPS):
            if turn:
                gram = contract_last(low(iterate), low(iterate))
            gram_low = low(gram)
            poly = low(ns_second * gram + ns_third * dot(gram_low, gram_low))
            if turn:
                iterate = ns_first * iterate + dot(poly, low(iterate))
            else:
                iterate = scale * (ns_first * wide + dot(poly, low(full)))
        change = step_size * iterate
        direction[slot] = change
        wnew[mat] = low(w[mat].reshape(hidden, width).astype(jnp.float32) - change)
        new_rows[mat] = state[mat] - direction[slot, own, :]

    orthogonalize(core, 0)
    sibling_seq = z * plane + sibling
    theirs = pl.ds(pl.multiple_of(sibling_seq * state_rows, state_rows), state_rows)
    swaps = [
        send(wnew.at[core], wnew.at[core], fresh_sem, (0,), device(z, sibling)),
        send(direction.at[0, theirs], moved, fresh_sem, (1,), device(z, sibling)),
    ]
    for step in range(planes):
        arrived(g.at[SHARED, z, p], gs_sem, (2, 0, step))
        for turn in range(1, rows_y):
            for kind in range(2):
                arrived(g.at[SHARED, z, p], gy_sem, (SHARED + kind, turn, step))
    orthogonalize(SHARED, 1)
    for level in range(1, back + 1):
        for copy in ups[level]:
            pl.when(z >= level)(copy.wait_recv)
    logs = [own_l[...]]
    for level in range(1, back + 1):
        row = jnp.broadcast_to(l_from[level - 1], (tokens, tokens))
        logs.append(row.T[:, :1])
    top = functools.reduce(jnp.maximum, logs)
    shares = [jnp.exp(log - top) for log in logs]
    attention = shares[0] * own_o[...]
    for level in range(1, back + 1):
        attention = attention + shares[level] * o_from[level - 1].astype(jnp.float32)
    attention = attention / functools.reduce(jnp.add, shares)
    for copy in swaps:
        copy.wait_recv()
    new_rows[1 - core] = state[1 - core] - moved[...]
    local_new = local(new_rows, new, 1)
    gate = contract_last(query_norm, wnew[0])
    active = low(gate * jax.nn.sigmoid(gate) * contract_last(query_norm, wnew[1]))
    comb[...] = low(attention + dot(active, wnew[SHARED]))

    o_copies = []
    for step in range(1, heads):
        target = lax.rem(head + step, heads)
        rows = pl.ds(pl.multiple_of(target * part, part), part)
        o_copies.append(
            send(comb.at[rows], out.at[:, own_columns], o_sem, (step,), head_peer(step))
        )
    local_out = local(comb.at[own_rows], out.at[:, own_columns], 0)
    local_out.wait()
    local_new.wait()
    for copy in o_copies:
        copy.wait_recv()
    drain()


def hand_over(combined, new_state, combined_out, new_state_out, sems):
    first = pltpu.make_async_copy(combined, combined_out, sems.at[0])
    second = pltpu.make_async_copy(new_state, new_state_out, sems.at[1])
    first.start()
    second.start()
    first.wait()
    second.wait()


def held(values):
    return pltpu.with_memory_space_constraint(values, pltpu.HBM)


def shards(sizes, qkv, token_rate, head_rate, fast_state):
    heads, planes, plane, back = sizes
    part, width = qkv.shape[1], qkv.shape[2] // heads
    tokens = token_rate.shape[0]
    state_rows = fast_state.shape[2]
    hidden = state_rows * planes * plane
    rows_y = plane // CORES
    levels = max(back, 1)
    link = jnp.bfloat16 if state_rows % 16 == 0 else jnp.float32
    dma = pltpu.SemaphoreType.DMA
    hbm = pl.BlockSpec(memory_space=pltpu.HBM)
    combined, new_state = pl.pallas_call(
        functools.partial(kernel, sizes),
        name="block",
        out_shape=(
            jax.ShapeDtypeStruct((part, heads * width), jnp.bfloat16),
            jax.ShapeDtypeStruct((MATS, state_rows, width), jnp.float32),
        ),
        in_specs=[hbm] * 4,
        out_specs=(hbm, hbm),
        scratch_shapes=[
            pltpu.VMEM((MATS, state_rows, width), jnp.float32),
            pltpu.SMEM((1,), jnp.float32),
            pltpu.VMEM((state_rows, width), jnp.float32),
            pltpu.VMEM((MATS, state_rows, width), jnp.float32),
            pltpu.VMEM((1, 2, plane, tokens, width), jnp.bfloat16),
            pltpu.VMEM((tokens, width), jnp.bfloat16),
            pltpu.VMEM((levels, tokens, width), jnp.bfloat16),
            pltpu.VMEM((levels, tokens, width), jnp.bfloat16),
            pltpu.VMEM((levels, tokens, width), jnp.bfloat16),
            pltpu.VMEM((levels, 1, tokens), jnp.float32),
            pltpu.VMEM((levels, 1, tokens), jnp.float32),
            pltpu.VMEM((MATS, planes, plane, state_rows, width), link),
            pltpu.VMEM((MATS, planes, state_rows, width), jnp.float32),
            pltpu.VMEM((MATS, planes, state_rows, width), link),
            pltpu.VMEM((MATS, planes - 1, state_rows, width), link),
            pltpu.VMEM((MATS, planes, plane, state_rows, width), link),
            pltpu.VMEM((MATS, hidden, width), jnp.bfloat16),
            pltpu.VMEM((2, hidden, width), jnp.float32),
            pltpu.VMEM((plane, 1, tokens), jnp.float32),
            pltpu.VMEM((tokens, width), jnp.bfloat16),
            pltpu.VMEM((tokens, width), jnp.float32),
            pltpu.VMEM((tokens, 1), jnp.float32),
            dma((5,)),
            dma((2, heads)),
            dma((2, plane)),
            dma((2, rows_y, heads)),
            dma((2, rows_y, heads)),
            dma((2, planes)),
            dma((2, MATS, rows_y)),
            dma((2, MATS, rows_y)),
            dma((2, 2, planes)),
            dma((2, MATS, planes)),
            dma((2, MATS + 1, rows_y, planes)),
            dma((2, MATS, rows_y, planes)),
            dma((2, back + 1)),
            dma((2, back + 1)),
            dma((2, back + 1)),
            dma((2, heads)),
            dma((2, 2)),
        ],
        compiler_params=pltpu.CompilerParams(
            collective_id=0, has_side_effects=True, vmem_limit_bytes=48 * 1024 * 1024
        ),
    )(
        held(qkv), held(token_rate.reshape(1, tokens)), head_rate, held(fast_state[:, 0])
    )
    return combined, new_state[:, None]


def solution(mesh):
    count, heads = mesh.shape["seq"], mesh.shape["head"]
    plane = CORES
    while plane * plane < count:
        plane *= 2
    planes = count // plane

    def whole(qkv, token_rate, head_rate, fast_state):
        plane_tokens = token_rate.shape[0] // planes
        back = min(-(-(WINDOW - 1) // plane_tokens), planes - 1)
        return jax.shard_map(
            functools.partial(shards, (heads, planes, plane, back)),
            mesh=mesh,
            in_specs=(
                P(None, ("seq", "head"), None),
                P("seq", "head"),
                P("head"),
                P(None, "head", "seq", None),
            ),
            out_specs=(P(("seq", "head"), None), P(None, "head", "seq", None)),
            check_vma=False,
        )(qkv, token_rate, head_rate, fast_state)

    return whole
```

```python
import functools

import jax
import jax.numpy as jnp
from jax import lax
from jax.experimental import pallas as pl
from jax.experimental.pallas import tpu as pltpu
from jax.sharding import PartitionSpec as P

WINDOW = 1024
NS_STEPS = 2

ns_first = 3.4445
ns_second = -4.775
ns_third = 2.0315
rms_eps = 1e-06
norm_eps = 1e-07
lowest = -1e30

MESH = pl.DeviceIdType.MESH
CORES = 2
MATS = 3
SHARED = 2


def rms_scaled(values):
    return values * lax.rsqrt(jnp.mean(values * values, axis=-1, keepdims=True) + rms_eps)


def contract_last(left_side, right_side):
    return lax.dot_general(
        left_side, right_side, (((1,), (1,)), ((), ())), preferred_element_type=jnp.float32
    )


def low(values):
    return values.astype(jnp.bfloat16)


def dot(left_side, right_side):
    return jnp.dot(left_side, right_side, preferred_element_type=jnp.float32)


def kernel(
    sizes,
    qkv, rate, head_rate, state_hbm,
    out, new,
    state, step_smem, moved, new_rows, kv, q, q_from, o_send, o_from, l_send, l_from, w,
    gfull, gsend, grecv, g, wnew, direction, rates, comb, own_o, own_l,
    local_sem, q_sem, rate_sem, ky_sem, ks_sem, wz_sem, wy_sem, ws_sem,
    rs_sem, gz_sem, gy_sem, gs_sem, down_sem, up_sem, log_sem, o_sem, fresh_sem,
):
    heads, planes, plane, back = sizes
    rows_y = plane // CORES
    part = qkv.shape[1]
    tokens, width = q.shape
    hidden = direction.shape[1]
    state_rows = state.shape[1]
    link = w.dtype
    count = plane * tokens

    seq = lax.axis_index("seq")
    head = lax.axis_index("head")
    z = seq // plane
    p = lax.rem(seq, plane)
    y = p // CORES
    core = lax.rem(p, CORES)
    sibling = y * CORES + (1 - core)

    def device(z_at, p_at):
        return {"seq": z_at * plane + p_at, "head": head}

    def wrap(z_at):
        return lax.rem(z_at + 2 * planes, planes)

    def p_of_y(step, kind=0):
        return lax.rem(y + step, rows_y) * CORES + (1 - core if kind else core)

    def head_peer(step):
        return {"seq": seq, "head": lax.rem(head + step, heads)}

    def guarded(when, action):
        if when is None:
            action()
        else:
            pl.when(when)(action)

    def far_peer(turn, step):
        return {"seq": z * plane + p_of_y(turn), "head": lax.rem(head + step, heads)}

    far = [(turn, step) for turn in range(rows_y) for step in range(heads) if turn + step]
    peers = [far_peer(turn, step) for turn, step in far if step]
    peers += [device(z, lax.rem(p + step, plane)) for step in range(1, plane)]
    peers += [device(wrap(z + step), at) for step in range(1, planes) for at in (p, sibling)]
    barrier = pltpu.get_barrier_semaphore()
    for peer in peers:
        pl.semaphore_signal(barrier, inc=1, device_id=peer, device_id_type=MESH)

    def local(src, dst, index):
        copy = pltpu.make_async_copy(src, dst, local_sem.at[index])
        copy.start()
        return copy

    state_copy = local(state_hbm, state, 0)
    rate_copy = local(rate, rates.at[p], 1)
    step_copy = local(head_rate, step_smem, 2)

    started = []

    def send(src, dst, sem, place, target, when=None):
        copy = pltpu.make_async_remote_copy(
            src_ref=src,
            dst_ref=dst,
            send_sem=sem.at[(0,) + place],
            recv_sem=sem.at[(1,) + place],
            device_id=target,
            device_id_type=MESH,
        )
        guarded(when, copy.start)
        started.append((copy, when))
        return copy

    def arrived(ref, sem, place):
        pltpu.make_async_remote_copy(
            src_ref=ref,
            dst_ref=ref,
            send_sem=sem.at[(0,) + place],
            recv_sem=sem.at[(1,) + place],
            device_id=device(z, sibling),
            device_id_type=MESH,
        ).wait_recv()

    def part_rows(step):
        owner = lax.rem(head - step + heads, heads)
        return pl.ds(pl.multiple_of(owner * part, part), part)

    def head_columns(index):
        return pl.ds(pl.multiple_of(index * width, width), width)

    own_rows = part_rows(0)
    own_columns = head_columns(head)
    for level in range(1, back + 1):
        @pl.when(z < level)
        def _(level=level):
            o_from[level - 1] = jnp.zeros_like(o_from[level - 1])
            l_from[level - 1] = jnp.full_like(l_from[level - 1], lowest)
    state_copy.wait()
    for mat in range(MATS):
        w[mat, z, p] = state[mat].astype(link)
    pl.semaphore_wait(barrier, len(peers))

    lower = 1 - z * 2 // planes
    near_first = [step + (planes - 2 * step) * lower for step in range(1, planes)]
    wz_copies = [
        send(w.at[:, z, p], w.at[:, z, p], wz_sem, (step,), device(wrap(z + step), p))
        for step in near_first
    ]

    local_q = local(qkv.at[0, :, own_columns], q.at[own_rows], 4)
    k_copies = {}
    for turn, step in sorted(far, key=lambda at: (at[1] == 0, -at[0])):
        k_copies[turn, step] = send(
            qkv.at[pl.ds(1, 2), :, head_columns(lax.rem(head + step, heads))],
            kv.at[0, :, p, own_rows],
            ky_sem, (turn, step), far_peer(turn, step),
        )
    q_copies = [
        send(
            qkv.at[0, :, head_columns(lax.rem(head + step, heads))],
            q.at[own_rows],
            q_sem, (step,), head_peer(step),
        )
        for step in range(1, heads)
    ]
    own_kv = qkv.at[pl.ds(1, 2), :, own_columns]
    ks_copies = {
        (0, 0): send(own_kv, kv.at[0, :, p, own_rows], ks_sem, (0, 0), device(z, sibling))
    }
    local_kv = local(own_kv, kv.at[0, :, p, own_rows], 3)
    rate_copy.wait()
    rate_copies = [
        send(rates.at[p], rates.at[p], rate_sem, (step,), device(z, lax.rem(p + step, plane)))
        for step in range(1, plane)
    ]
    for turn, step in far:
        k_copies[turn, step].wait_recv()
        block = kv.at[0, :, p_of_y(rows_y - turn), part_rows(step)]
        ks_copies[turn, step] = send(block, block, ks_sem, (turn, step), device(z, sibling))
    local_q.wait()
    for copy in q_copies:
        copy.wait_recv()

    downs = {}

    def descend(level):
        src = q if level == 1 else q_from.at[level - 2]
        when = (z >= 1) & (z + level - 1 < planes)
        downs[level] = send(
            src, q_from.at[level - 1], down_sem, (level,), device(wrap(z - 1), p), when
        )

    if back >= 1:
        descend(1)
    local_kv.wait()
    for copy in wz_copies + rate_copies:
        copy.wait_recv()
    column = [
        low(w[mat, :, p].reshape(planes * state_rows, width)) for mat in range(MATS)
    ]

    def gradients(kind):
        places = [p_of_y(turn, kind) for turn in range(rows_y)]
        keys = jnp.concatenate([kv[0, 0, place] for place in places], axis=0)
        values = jnp.concatenate([kv[0, 1, place] for place in places], axis=0)
        rate_row = -jnp.concatenate([rates[place] for place in places], axis=1)
        key_norm = low(rms_scaled(keys.astype(jnp.float32)))
        gate_act = contract_last(column[0], key_norm)
        up_act = contract_last(column[1], key_norm)
        back_grad = contract_last(column[2], values) * rate_row
        sigmoid_gate = jax.nn.sigmoid(gate_act)
        silu_gate = gate_act * sigmoid_gate
        grad_gate = back_grad * up_act * sigmoid_gate * (1.0 + gate_act * (1.0 - sigmoid_gate))
        lefts = (grad_gate, back_grad * silu_gate, silu_gate * up_act * rate_row)
        for mat in range(MATS):
            total = dot(low(lefts[mat]), values if mat == SHARED else key_norm)
            yield total.reshape(planes, state_rows, width)

    for mat, total in enumerate(gradients(0)):
        gfull[mat] = total
    for copy in ks_copies.values():
        copy.wait_recv()

    groups = (pl.ds(0, SHARED), pl.ds(SHARED, 1))
    for mat, total in enumerate(gradients(1)):
        total = total + gfull[mat]
        gfull[mat] = total
        gsend[mat] = total.astype(link)
        if mat:
            group = mat - 1
            for step in near_first:
                send(
                    gsend.at[groups[group], wrap(z + step)], grecv.at[groups[group], step - 1],
                    rs_sem, (group, step), device(wrap(z + step), p),
                )

    def attend(level):
        queries = q[...] if level == 0 else q_from[level - 1]
        scores = contract_last(queries, kv[0, 0].reshape(count, width)) * width ** (-0.5)
        query_pos = level * count + p * tokens + lax.broadcasted_iota(jnp.int32, scores.shape, 0)
        key_pos = lax.broadcasted_iota(jnp.int32, scores.shape, 1)
        visible = (key_pos <= query_pos) & (key_pos > query_pos - WINDOW)
        scores = jnp.where(visible, scores, -jnp.inf)
        row_max = jnp.maximum(jnp.max(scores, axis=1, keepdims=True), lowest)
        exp_scores = jnp.exp(scores - row_max)
        row_sum = jnp.sum(exp_scores, axis=1, keepdims=True)
        result = dot(low(exp_scores), kv[0, 1].reshape(count, width))
        result = result / jnp.maximum(row_sum, 1e-30)
        log_sum = jnp.where(row_sum > 0.0, row_max + jnp.log(jnp.maximum(row_sum, 1e-30)), lowest)
        if level == 0:
            own_o[...] = result
            own_l[...] = log_sum
        else:
            o_send[level - 1] = low(result)
            l_send[level - 1] = jnp.broadcast_to(log_sum, (tokens, tokens)).T[:1]

    def w_at(mat, p_at):
        return w.at[mat, :, p_at]

    w_copies = {}
    for turn in range(1, rows_y):
        for kind, mat in ((0, core), (1, 1 - core), (2, SHARED)):
            w_copies[kind, turn] = send(
                w_at(mat, p), w_at(mat, p), wy_sem, (kind, turn), device(z, p_of_y(turn, kind % 2))
            )
    for kind, mat in ((1, 1 - core), (2, SHARED)):
        w_copies[kind, 0] = send(
            w_at(mat, p), w_at(mat, p), ws_sem, (kind, 0), device(z, sibling)
        )
    attend(0)

    def attend_for(level):
        @pl.when(z + level < planes)
        def _():
            if level > 1:
                downs[level].wait_recv()
            attend(level)

    ups = {}

    def ascend(level):
        when = z + level < planes
        target = device(wrap(z + level), p)
        ups[level] = (
            send(o_send.at[level - 1], o_from.at[level - 1], up_sem, (level,), target, when),
            send(l_send.at[level - 1], l_from.at[level - 1], log_sem, (level,), target, when),
        )

    if back >= 1:
        pl.when(z + 1 < planes)(downs[1].wait_recv)
    if back >= 1:
        attend_for(1)

    def drain():
        for copy, when in started:
            guarded(when, copy.wait_send)
        started.clear()

    def rs_sum(group):
        places = groups[group]
        total = gfull[places, z]
        for step in near_first:
            arrived(gsend.at[places, z], rs_sem, (group, step))
        for step in range(1, planes):
            total = total + grecv[places, step - 1].astype(jnp.float32)
        g[places, z, p] = total.astype(link)

    def pass_on(piece, sem, place, target):
        return send(piece, piece, sem, place, target)

    rs_sum(0)
    for step in near_first:
        for kind, mat, at in ((0, core, p), (1, 1 - core, sibling)):
            pass_on(g.at[mat, z, p], gz_sem, (kind, step), device(wrap(z + step), at))
    for turn in range(1, rows_y):
        for kind, mat in ((0, core), (1, 1 - core)):
            pass_on(g.at[mat, z, p], gy_sem, (kind, turn, 0), device(z, p_of_y(turn, kind)))
    pass_on(g.at[1 - core, z, p], gs_sem, (1, 0, 0), device(z, sibling))

    def shared_on(step):
        piece = g.at[SHARED, wrap(z - step), p]
        for turn in range(1, rows_y):
            for kind in range(2):
                target = device(z, p_of_y(turn, kind))
                pass_on(piece, gy_sem, (SHARED + kind, turn, step), target)
        pass_on(piece, gs_sem, (2, 0, step), device(z, sibling))

    if back >= 2:
        descend(2)
    rs_sum(1)
    for step in near_first:
        pass_on(g.at[SHARED, z, p], gz_sem, (2, step), device(wrap(z + step), p))
    shared_on(0)
    if back >= 1:
        ascend(1)

    for step in near_first:
        for kind, at in ((0, p), (1, sibling)):
            piece = g.at[core, wrap(z - step), at]
            arrived(piece, gz_sem, (kind, step))
            for turn in range(1, rows_y):
                pass_on(piece, gy_sem, (kind, turn, step), device(z, p_of_y(turn)))
    for level in range(2, back + 1):
        attend_for(level)
        ascend(level)
        if level < back:
            descend(level + 1)
    for turn in range(1, rows_y):
        w_copies[2, turn].wait_recv()
        piece = w_at(SHARED, p_of_y(rows_y - turn))
        w_copies[3, turn] = send(piece, piece, ws_sem, (2, turn), device(z, sibling))
    query_norm = low(rms_scaled(q[...].astype(jnp.float32)))

    def shared_take(step):
        arrived(g.at[SHARED, wrap(z - step), p], gz_sem, (2, step))
        shared_on(step)

    for step in near_first:
        shared_take(step)
    for key, copy in w_copies.items():
        if key not in [(2, turn) for turn in range(1, rows_y)]:
            copy.wait_recv()
    arrived(g.at[core, z, p], gs_sem, (1, 0, 0))
    for step in range(planes):
        for turn in range(1, rows_y):
            for kind in range(2):
                arrived(g.at[core, z, p], gy_sem, (kind, turn, step))

    step_copy.wait()
    step_size = step_smem[0]
    own = pl.ds(pl.multiple_of(seq * state_rows, state_rows), state_rows)

    def orthogonalize(mat, slot):
        full = g[mat].reshape(hidden, width)
        wide = full.astype(jnp.float32)
        scale = 1.0 / (jnp.sqrt(jnp.sum(wide * wide)) + norm_eps)
        gram = contract_last(low(full), low(full)) * (scale * scale)
        iterate = None
        for turn in range(NS_STEPS):
            if turn:
                gram = contract_last(low(iterate), low(iterate))
            gram_low = low(gram)
            poly = low(ns_second * gram + ns_third * dot(gram_low, gram_low))
            if turn:
                iterate = ns_first * iterate + dot(poly, low(iterate))
            else:
                iterate = scale * (ns_first * wide + dot(poly, low(full)))
        change = step_size * iterate
        direction[slot] = change
        wnew[mat] = low(w[mat].reshape(hidden, width).astype(jnp.float32) - change)
        new_rows[mat] = state[mat] - direction[slot, own, :]

    orthogonalize(core, 0)
    sibling_seq = z * plane + sibling
    theirs = pl.ds(pl.multiple_of(sibling_seq * state_rows, state_rows), state_rows)
    swaps = [
        send(wnew.at[core], wnew.at[core], fresh_sem, (0,), device(z, sibling)),
        send(direction.at[0, theirs], moved, fresh_sem, (1,), device(z, sibling)),
    ]
    for step in range(planes):
        arrived(g.at[SHARED, z, p], gs_sem, (2, 0, step))
        for turn in range(1, rows_y):
            for kind in range(2):
                arrived(g.at[SHARED, z, p], gy_sem, (SHARED + kind, turn, step))
    orthogonalize(SHARED, 1)
    for level in range(1, back + 1):
        for copy in ups[level]:
            pl.when(z >= level)(copy.wait_recv)
    logs = [own_l[...]]
    for level in range(1, back + 1):
        row = jnp.broadcast_to(l_from[level - 1], (tokens, tokens))
        logs.append(row.T[:, :1])
    top = functools.reduce(jnp.maximum, logs)
    shares = [jnp.exp(log - top) for log in logs]
    attention = shares[0] * own_o[...]
    for level in range(1, back + 1):
        attention = attention + shares[level] * o_from[level - 1].astype(jnp.float32)
    attention = attention / functools.reduce(jnp.add, shares)
    for copy in swaps:
        copy.wait_recv()
    new_rows[1 - core] = state[1 - core] - moved[...]
    local_new = local(new_rows, new, 1)
    gate = contract_last(query_norm, wnew[0])
    active = low(gate * jax.nn.sigmoid(gate) * contract_last(query_norm, wnew[1]))
    comb[...] = low(attention + dot(active, wnew[SHARED]))

    o_copies = []
    for step in range(1, heads):
        target = lax.rem(head + step, heads)
        rows = pl.ds(pl.multiple_of(target * part, part), part)
        o_copies.append(
            send(comb.at[rows], out.at[:, own_columns], o_sem, (step,), head_peer(step))
        )
    local_out = local(comb.at[own_rows], out.at[:, own_columns], 0)
    local_out.wait()
    local_new.wait()
    for copy in o_copies:
        copy.wait_recv()
    drain()


def hand_over(combined, new_state, combined_out, new_state_out, sems):
    first = pltpu.make_async_copy(combined, combined_out, sems.at[0])
    second = pltpu.make_async_copy(new_state, new_state_out, sems.at[1])
    first.start()
    second.start()
    first.wait()
    second.wait()


def held(values):
    return pltpu.with_memory_space_constraint(values, pltpu.HBM)


def shards(sizes, qkv, token_rate, head_rate, fast_state):
    heads, planes, plane, back = sizes
    part, width = qkv.shape[1], qkv.shape[2] // heads
    tokens = token_rate.shape[0]
    state_rows = fast_state.shape[2]
    hidden = state_rows * planes * plane
    rows_y = plane // CORES
    levels = max(back, 1)
    link = jnp.bfloat16 if state_rows % 16 == 0 else jnp.float32
    dma = pltpu.SemaphoreType.DMA
    hbm = pl.BlockSpec(memory_space=pltpu.HBM)
    combined, new_state = pl.pallas_call(
        functools.partial(kernel, sizes),
        name="block",
        out_shape=(
            jax.ShapeDtypeStruct((part, heads * width), jnp.bfloat16),
            jax.ShapeDtypeStruct((MATS, state_rows, width), jnp.float32),
        ),
        in_specs=[hbm] * 4,
        out_specs=(hbm, hbm),
        scratch_shapes=[
            pltpu.VMEM((MATS, state_rows, width), jnp.float32),
            pltpu.SMEM((1,), jnp.float32),
            pltpu.VMEM((state_rows, width), jnp.float32),
            pltpu.VMEM((MATS, state_rows, width), jnp.float32),
            pltpu.VMEM((1, 2, plane, tokens, width), jnp.bfloat16),
            pltpu.VMEM((tokens, width), jnp.bfloat16),
            pltpu.VMEM((levels, tokens, width), jnp.bfloat16),
            pltpu.VMEM((levels, tokens, width), jnp.bfloat16),
            pltpu.VMEM((levels, tokens, width), jnp.bfloat16),
            pltpu.VMEM((levels, 1, tokens), jnp.float32),
            pltpu.VMEM((levels, 1, tokens), jnp.float32),
            pltpu.VMEM((MATS, planes, plane, state_rows, width), link),
            pltpu.VMEM((MATS, planes, state_rows, width), jnp.float32),
            pltpu.VMEM((MATS, planes, state_rows, width), link),
            pltpu.VMEM((MATS, planes - 1, state_rows, width), link),
            pltpu.VMEM((MATS, planes, plane, state_rows, width), link),
            pltpu.VMEM((MATS, hidden, width), jnp.bfloat16),
            pltpu.VMEM((2, hidden, width), jnp.float32),
            pltpu.VMEM((plane, 1, tokens), jnp.float32),
            pltpu.VMEM((tokens, width), jnp.bfloat16),
            pltpu.VMEM((tokens, width), jnp.float32),
            pltpu.VMEM((tokens, 1), jnp.float32),
            dma((5,)),
            dma((2, heads)),
            dma((2, plane)),
            dma((2, rows_y, heads)),
            dma((2, rows_y, heads)),
            dma((2, planes)),
            dma((2, MATS, rows_y)),
            dma((2, MATS, rows_y)),
            dma((2, 2, planes)),
            dma((2, MATS, planes)),
            dma((2, MATS + 1, rows_y, planes)),
            dma((2, MATS, rows_y, planes)),
            dma((2, back + 1)),
            dma((2, back + 1)),
            dma((2, back + 1)),
            dma((2, heads)),
            dma((2, 2)),
        ],
        compiler_params=pltpu.CompilerParams(
            collective_id=0, has_side_effects=True, vmem_limit_bytes=48 * 1024 * 1024
        ),
    )(
        held(qkv), held(token_rate.reshape(1, tokens)), head_rate, held(fast_state[:, 0])
    )
    return combined, new_state[:, None]


def solution(mesh):
    count, heads = mesh.shape["seq"], mesh.shape["head"]
    plane = CORES
    while plane * plane < count:
        plane *= 2
    planes = count // plane

    def whole(qkv, token_rate, head_rate, fast_state):
        plane_tokens = token_rate.shape[0] // planes
        back = min(-(-(WINDOW - 1) // plane_tokens), planes - 1)
        return jax.shard_map(
            functools.partial(shards, (heads, planes, plane, back)),
            mesh=mesh,
            in_specs=(
                P(None, ("seq", "head"), None),
                P("seq", "head"),
                P("head"),
                P(None, "head", "seq", None),
            ),
            out_specs=(P(("seq", "head"), None), P(None, "head", "seq", None)),
            check_vma=False,
        )(qkv, token_rate, head_rate, fast_state)

    return whole
```

```python
import functools

import jax
import jax.numpy as jnp
from jax import lax
from jax.experimental import pallas as pl
from jax.experimental.pallas import tpu as pltpu
from jax.sharding import PartitionSpec as P

WINDOW = 1024
NS_STEPS = 2

ns_first = 3.4445
ns_second = -4.775
ns_third = 2.0315
rms_eps = 1e-06
norm_eps = 1e-07
lowest = -1e30

MESH = pl.DeviceIdType.MESH
CORES = 2
MATS = 3
SHARED = 2


def rms_scaled(values):
    return values * lax.rsqrt(jnp.mean(values * values, axis=-1, keepdims=True) + rms_eps)


def contract_last(left_side, right_side):
    return lax.dot_general(
        left_side, right_side, (((1,), (1,)), ((), ())), preferred_element_type=jnp.float32
    )


def low(values):
    return values.astype(jnp.bfloat16)


def dot(left_side, right_side):
    return jnp.dot(left_side, right_side, preferred_element_type=jnp.float32)


def kernel(
    sizes,
    qkv, rate, head_rate, state_hbm,
    out, new,
    state, step_smem, moved, new_rows, kv, q, q_from, o_send, o_from, l_send, l_from, w,
    gfull, gsend, grecv, g, wnew, direction, rates, comb, own_o, own_l, act,
    local_sem, q_sem, rate_sem, ky_sem, ks_sem, wz_sem, wy_sem, ws_sem,
    rs_sem, gz_sem, gy_sem, gs_sem, down_sem, up_sem, log_sem, o_sem, fresh_sem,
):
    heads, planes, plane, back = sizes
    rows_y = plane // CORES
    part = qkv.shape[1]
    tokens, width = q.shape
    hidden = direction.shape[1]
    state_rows = state.shape[1]
    link = w.dtype
    count = plane * tokens

    seq = lax.axis_index("seq")
    head = lax.axis_index("head")
    z = seq // plane
    p = lax.rem(seq, plane)
    y = p // CORES
    core = lax.rem(p, CORES)
    sibling = y * CORES + (1 - core)

    def device(z_at, p_at):
        return {"seq": z_at * plane + p_at, "head": head}

    def wrap(z_at):
        return lax.rem(z_at + 2 * planes, planes)

    def p_of_y(step, kind=0):
        return lax.rem(y + step, rows_y) * CORES + (1 - core if kind else core)

    def head_peer(step):
        return {"seq": seq, "head": lax.rem(head + step, heads)}

    def guarded(when, action):
        if when is None:
            action()
        else:
            pl.when(when)(action)

    def far_peer(turn, step):
        return {"seq": z * plane + p_of_y(turn), "head": lax.rem(head + step, heads)}

    far = [(turn, step) for turn in range(rows_y) for step in range(heads) if turn + step]
    peers = [far_peer(turn, step) for turn, step in far if step]
    peers += [device(z, lax.rem(p + step, plane)) for step in range(1, plane)]
    peers += [device(wrap(z + step), at) for step in range(1, planes) for at in (p, sibling)]
    barrier = pltpu.get_barrier_semaphore()
    for peer in peers:
        pl.semaphore_signal(barrier, inc=1, device_id=peer, device_id_type=MESH)

    def local(src, dst, index):
        copy = pltpu.make_async_copy(src, dst, local_sem.at[index])
        copy.start()
        return copy

    state_copy = local(state_hbm, state, 0)
    rate_copy = local(rate, rates.at[p], 1)
    step_copy = local(head_rate, step_smem, 2)

    started = []

    def send(src, dst, sem, place, target, when=None):
        copy = pltpu.make_async_remote_copy(
            src_ref=src,
            dst_ref=dst,
            send_sem=sem.at[(0,) + place],
            recv_sem=sem.at[(1,) + place],
            device_id=target,
            device_id_type=MESH,
        )
        guarded(when, copy.start)
        started.append((copy, when))
        return copy

    def arrived(ref, sem, place):
        pltpu.make_async_remote_copy(
            src_ref=ref,
            dst_ref=ref,
            send_sem=sem.at[(0,) + place],
            recv_sem=sem.at[(1,) + place],
            device_id=device(z, sibling),
            device_id_type=MESH,
        ).wait_recv()

    def part_rows(step):
        owner = lax.rem(head - step + heads, heads)
        return pl.ds(pl.multiple_of(owner * part, part), part)

    def head_columns(index):
        return pl.ds(pl.multiple_of(index * width, width), width)

    own_rows = part_rows(0)
    own_columns = head_columns(head)
    for level in range(1, back + 1):
        @pl.when(z < level)
        def _(level=level):
            o_from[level - 1] = jnp.zeros_like(o_from[level - 1])
            l_from[level - 1] = jnp.full_like(l_from[level - 1], lowest)
    state_copy.wait()
    for mat in range(MATS):
        w[mat, z, p] = state[mat].astype(link)
    pl.semaphore_wait(barrier, len(peers))

    lower = 1 - z * 2 // planes
    near_first = [step + (planes - 2 * step) * lower for step in range(1, planes)]
    wz_copies = [
        send(w.at[:, z, p], w.at[:, z, p], wz_sem, (step,), device(wrap(z + step), p))
        for step in near_first
    ]

    local_q = local(qkv.at[0, :, own_columns], q.at[own_rows], 4)
    k_copies = {}
    for turn, step in sorted(far, key=lambda at: (at[1] == 0, -at[0])):
        k_copies[turn, step] = send(
            qkv.at[pl.ds(1, 2), :, head_columns(lax.rem(head + step, heads))],
            kv.at[0, :, p, own_rows],
            ky_sem, (turn, step), far_peer(turn, step),
        )
    q_copies = [
        send(
            qkv.at[0, :, head_columns(lax.rem(head + step, heads))],
            q.at[own_rows],
            q_sem, (step,), head_peer(step),
        )
        for step in range(1, heads)
    ]
    own_kv = qkv.at[pl.ds(1, 2), :, own_columns]
    ks_copies = {
        (0, 0): send(own_kv, kv.at[0, :, p, own_rows], ks_sem, (0, 0), device(z, sibling))
    }
    local_kv = local(own_kv, kv.at[0, :, p, own_rows], 3)
    rate_copy.wait()
    rate_copies = [
        send(rates.at[p], rates.at[p], rate_sem, (step,), device(z, lax.rem(p + step, plane)))
        for step in range(1, plane)
    ]
    for turn, step in far:
        k_copies[turn, step].wait_recv()
        block = kv.at[0, :, p_of_y(rows_y - turn), part_rows(step)]
        ks_copies[turn, step] = send(block, block, ks_sem, (turn, step), device(z, sibling))
    local_q.wait()
    for copy in q_copies:
        copy.wait_recv()

    downs = {}

    def descend(level):
        src = q if level == 1 else q_from.at[level - 2]
        when = (z >= 1) & (z + level - 1 < planes)
        downs[level] = send(
            src, q_from.at[level - 1], down_sem, (level,), device(wrap(z - 1), p), when
        )

    if back >= 1:
        descend(1)
    local_kv.wait()
    for copy in wz_copies + rate_copies:
        copy.wait_recv()
    column = [
        low(w[mat, :, p].reshape(planes * state_rows, width)) for mat in range(MATS)
    ]

    def gradients(kind):
        places = [p_of_y(turn, kind) for turn in range(rows_y)]
        keys = jnp.concatenate([kv[0, 0, place] for place in places], axis=0)
        values = jnp.concatenate([kv[0, 1, place] for place in places], axis=0)
        rate_row = -jnp.concatenate([rates[place] for place in places], axis=1)
        key_norm = low(rms_scaled(keys.astype(jnp.float32)))
        gate_act = contract_last(column[0], key_norm)
        up_act = contract_last(column[1], key_norm)
        back_grad = contract_last(column[2], values) * rate_row
        sigmoid_gate = jax.nn.sigmoid(gate_act)
        silu_gate = gate_act * sigmoid_gate
        grad_gate = back_grad * up_act * sigmoid_gate * (1.0 + gate_act * (1.0 - sigmoid_gate))
        lefts = (grad_gate, back_grad * silu_gate, silu_gate * up_act * rate_row)
        for mat in range(MATS):
            total = dot(low(lefts[mat]), values if mat == SHARED else key_norm)
            yield total.reshape(planes, state_rows, width)

    for mat, total in enumerate(gradients(0)):
        gfull[mat] = total
    for copy in ks_copies.values():
        copy.wait_recv()

    groups = (pl.ds(0, SHARED), pl.ds(SHARED, 1))
    for mat, total in enumerate(gradients(1)):
        total = total + gfull[mat]
        gfull[mat] = total
        gsend[mat] = total.astype(link)
        if mat:
            group = mat - 1
            for step in near_first:
                send(
                    gsend.at[groups[group], wrap(z + step)], grecv.at[groups[group], step - 1],
                    rs_sem, (group, step), device(wrap(z + step), p),
                )

    def attend(level):
        queries = q[...] if level == 0 else q_from[level - 1]
        scores = contract_last(queries, kv[0, 0].reshape(count, width)) * width ** (-0.5)
        query_pos = level * count + p * tokens + lax.broadcasted_iota(jnp.int32, scores.shape, 0)
        key_pos = lax.broadcasted_iota(jnp.int32, scores.shape, 1)
        visible = (key_pos <= query_pos) & (key_pos > query_pos - WINDOW)
        scores = jnp.where(visible, scores, -jnp.inf)
        row_max = jnp.maximum(jnp.max(scores, axis=1, keepdims=True), lowest)
        exp_scores = jnp.exp(scores - row_max)
        row_sum = jnp.sum(exp_scores, axis=1, keepdims=True)
        result = dot(low(exp_scores), kv[0, 1].reshape(count, width))
        result = result / jnp.maximum(row_sum, 1e-30)
        log_sum = jnp.where(row_sum > 0.0, row_max + jnp.log(jnp.maximum(row_sum, 1e-30)), lowest)
        if level == 0:
            own_o[...] = result
            own_l[...] = log_sum
        else:
            o_send[level - 1] = low(result)
            l_send[level - 1] = jnp.broadcast_to(log_sum, (tokens, tokens)).T[:1]

    def w_at(mat, p_at):
        return w.at[mat, :, p_at]

    w_copies = {}
    for turn in range(1, rows_y):
        for kind, mat in ((0, core), (1, 1 - core), (2, SHARED)):
            w_copies[kind, turn] = send(
                w_at(mat, p), w_at(mat, p), wy_sem, (kind, turn), device(z, p_of_y(turn, kind % 2))
            )
    for kind, mat in ((1, 1 - core), (2, SHARED)):
        w_copies[kind, 0] = send(
            w_at(mat, p), w_at(mat, p), ws_sem, (kind, 0), device(z, sibling)
        )
    attend(0)

    def attend_for(level):
        @pl.when(z + level < planes)
        def _():
            if level > 1:
                downs[level].wait_recv()
            attend(level)

    ups = {}

    def ascend(level):
        when = z + level < planes
        target = device(wrap(z + level), p)
        ups[level] = (
            send(o_send.at[level - 1], o_from.at[level - 1], up_sem, (level,), target, when),
            send(l_send.at[level - 1], l_from.at[level - 1], log_sem, (level,), target, when),
        )

    if back >= 1:
        pl.when(z + 1 < planes)(downs[1].wait_recv)
    if back >= 1:
        attend_for(1)

    def drain():
        for copy, when in started:
            guarded(when, copy.wait_send)
        started.clear()

    def rs_sum(group):
        places = groups[group]
        total = gfull[places, z]
        for step in near_first:
            arrived(gsend.at[places, z], rs_sem, (group, step))
        for step in range(1, planes):
            total = total + grecv[places, step - 1].astype(jnp.float32)
        g[places, z, p] = total.astype(link)

    def pass_on(piece, sem, place, target):
        return send(piece, piece, sem, place, target)

    rs_sum(0)
    for step in near_first:
        for kind, mat, at in ((0, core, p), (1, 1 - core, sibling)):
            pass_on(g.at[mat, z, p], gz_sem, (kind, step), device(wrap(z + step), at))
    for turn in range(1, rows_y):
        for kind, mat in ((0, core), (1, 1 - core)):
            pass_on(g.at[mat, z, p], gy_sem, (kind, turn, 0), device(z, p_of_y(turn, kind)))
    pass_on(g.at[1 - core, z, p], gs_sem, (1, 0, 0), device(z, sibling))

    def shared_on(step):
        piece = g.at[SHARED, wrap(z - step), p]
        for turn in range(1, rows_y):
            for kind in range(2):
                target = device(z, p_of_y(turn, kind))
                pass_on(piece, gy_sem, (SHARED + kind, turn, step), target)
        pass_on(piece, gs_sem, (2, 0, step), device(z, sibling))

    if back >= 2:
        descend(2)
    rs_sum(1)
    for step in near_first:
        pass_on(g.at[SHARED, z, p], gz_sem, (2, step), device(wrap(z + step), p))
    shared_on(0)
    if back >= 1:
        ascend(1)

    for step in near_first:
        for kind, at in ((0, p), (1, sibling)):
            piece = g.at[core, wrap(z - step), at]
            arrived(piece, gz_sem, (kind, step))
            for turn in range(1, rows_y):
                pass_on(piece, gy_sem, (kind, turn, step), device(z, p_of_y(turn)))
    for level in range(2, back + 1):
        attend_for(level)
        ascend(level)
        if level < back:
            descend(level + 1)
    for turn in range(1, rows_y):
        w_copies[2, turn].wait_recv()
        piece = w_at(SHARED, p_of_y(rows_y - turn))
        w_copies[3, turn] = send(piece, piece, ws_sem, (2, turn), device(z, sibling))
    query_norm = low(rms_scaled(q[...].astype(jnp.float32)))

    def shared_take(step):
        arrived(g.at[SHARED, wrap(z - step), p], gz_sem, (2, step))
        shared_on(step)

    for step in near_first:
        shared_take(step)
    for key, copy in w_copies.items():
        if key not in [(2, turn) for turn in range(1, rows_y)]:
            copy.wait_recv()
    arrived(g.at[core, z, p], gs_sem, (1, 0, 0))
    for step in range(planes):
        for turn in range(1, rows_y):
            for kind in range(2):
                arrived(g.at[core, z, p], gy_sem, (kind, turn, step))

    step_copy.wait()
    step_size = step_smem[0]
    own = pl.ds(pl.multiple_of(seq * state_rows, state_rows), state_rows)

    def orthogonalize(mat, slot):
        full = g[mat].reshape(hidden, width)
        wide = full.astype(jnp.float32)
        scale = 1.0 / (jnp.sqrt(jnp.sum(wide * wide)) + norm_eps)
        gram = contract_last(low(full), low(full)) * (scale * scale)
        iterate = None
        for turn in range(NS_STEPS):
            if turn:
                gram = contract_last(low(iterate), low(iterate))
            gram_low = low(gram)
            poly = low(ns_second * gram + ns_third * dot(gram_low, gram_low))
            if turn:
                iterate = ns_first * iterate + dot(poly, low(iterate))
            else:
                iterate = scale * (ns_first * wide + dot(poly, low(full)))
        change = step_size * iterate
        direction[slot] = change
        wnew[mat] = low(w[mat].reshape(hidden, width).astype(jnp.float32) - change)
        new_rows[mat] = state[mat] - direction[slot, own, :]

    orthogonalize(core, 0)
    sibling_seq = z * plane + sibling
    theirs = pl.ds(pl.multiple_of(sibling_seq * state_rows, state_rows), state_rows)
    swaps = [
        send(wnew.at[core], wnew.at[core], fresh_sem, (0,), device(z, sibling)),
        send(direction.at[0, theirs], moved, fresh_sem, (1,), device(z, sibling)),
    ]
    for step in range(planes):
        arrived(g.at[SHARED, z, p], gs_sem, (2, 0, step))
        for turn in range(1, rows_y):
            for kind in range(2):
                arrived(g.at[SHARED, z, p], gy_sem, (SHARED + kind, turn, step))
    orthogonalize(SHARED, 1)
    for level in range(1, back + 1):
        for copy in ups[level]:
            pl.when(z >= level)(copy.wait_recv)
    logs = [own_l[...]]
    for level in range(1, back + 1):
        row = jnp.broadcast_to(l_from[level - 1], (tokens, tokens))
        logs.append(row.T[:, :1])
    top = functools.reduce(jnp.maximum, logs)
    shares = [jnp.exp(log - top) for log in logs]
    attention = shares[0] * own_o[...]
    for level in range(1, back + 1):
        attention = attention + shares[level] * o_from[level - 1].astype(jnp.float32)
    attention = attention / functools.reduce(jnp.add, shares)
    for copy in swaps:
        copy.wait_recv()
    new_rows[1 - core] = state[1 - core] - moved[...]
    local_new = local(new_rows, new, 1)
    gate = contract_last(query_norm, wnew[0])
    act[...] = low(gate * jax.nn.sigmoid(gate) * contract_last(query_norm, wnew[1]))
    own_o[...] = attention

    def finish(rows):
        comb[rows] = low(own_o[rows] + dot(act[rows], wnew[SHARED]))

    o_copies = []
    for step in range(1, heads):
        target = lax.rem(head + step, heads)
        rows = pl.ds(pl.multiple_of(target * part, part), part)
        finish(rows)
        o_copies.append(
            send(comb.at[rows], out.at[:, own_columns], o_sem, (step,), head_peer(step))
        )
    finish(own_rows)
    local_out = local(comb.at[own_rows], out.at[:, own_columns], 0)
    local_out.wait()
    local_new.wait()
    for copy in o_copies:
        copy.wait_recv()
    drain()


def hand_over(combined, new_state, combined_out, new_state_out, sems):
    first = pltpu.make_async_copy(combined, combined_out, sems.at[0])
    second = pltpu.make_async_copy(new_state, new_state_out, sems.at[1])
    first.start()
    second.start()
    first.wait()
    second.wait()


def held(values):
    return pltpu.with_memory_space_constraint(values, pltpu.HBM)


def shards(sizes, qkv, token_rate, head_rate, fast_state):
    heads, planes, plane, back = sizes
    part, width = qkv.shape[1], qkv.shape[2] // heads
    tokens = token_rate.shape[0]
    state_rows = fast_state.shape[2]
    hidden = state_rows * planes * plane
    rows_y = plane // CORES
    levels = max(back, 1)
    link = jnp.bfloat16 if state_rows % 16 == 0 else jnp.float32
    dma = pltpu.SemaphoreType.DMA
    hbm = pl.BlockSpec(memory_space=pltpu.HBM)
    combined, new_state = pl.pallas_call(
        functools.partial(kernel, sizes),
        name="block",
        out_shape=(
            jax.ShapeDtypeStruct((part, heads * width), jnp.bfloat16),
            jax.ShapeDtypeStruct((MATS, state_rows, width), jnp.float32),
        ),
        in_specs=[hbm] * 4,
        out_specs=(hbm, hbm),
        scratch_shapes=[
            pltpu.VMEM((MATS, state_rows, width), jnp.float32),
            pltpu.SMEM((1,), jnp.float32),
            pltpu.VMEM((state_rows, width), jnp.float32),
            pltpu.VMEM((MATS, state_rows, width), jnp.float32),
            pltpu.VMEM((1, 2, plane, tokens, width), jnp.bfloat16),
            pltpu.VMEM((tokens, width), jnp.bfloat16),
            pltpu.VMEM((levels, tokens, width), jnp.bfloat16),
            pltpu.VMEM((levels, tokens, width), jnp.bfloat16),
            pltpu.VMEM((levels, tokens, width), jnp.bfloat16),
            pltpu.VMEM((levels, 1, tokens), jnp.float32),
            pltpu.VMEM((levels, 1, tokens), jnp.float32),
            pltpu.VMEM((MATS, planes, plane, state_rows, width), link),
            pltpu.VMEM((MATS, planes, state_rows, width), jnp.float32),
            pltpu.VMEM((MATS, planes, state_rows, width), link),
            pltpu.VMEM((MATS, planes - 1, state_rows, width), link),
            pltpu.VMEM((MATS, planes, plane, state_rows, width), link),
            pltpu.VMEM((MATS, hidden, width), jnp.bfloat16),
            pltpu.VMEM((2, hidden, width), jnp.float32),
            pltpu.VMEM((plane, 1, tokens), jnp.float32),
            pltpu.VMEM((tokens, width), jnp.bfloat16),
            pltpu.VMEM((tokens, width), jnp.float32),
            pltpu.VMEM((tokens, 1), jnp.float32),
            pltpu.VMEM((tokens, hidden), jnp.bfloat16),
            dma((5,)),
            dma((2, heads)),
            dma((2, plane)),
            dma((2, rows_y, heads)),
            dma((2, rows_y, heads)),
            dma((2, planes)),
            dma((2, MATS, rows_y)),
            dma((2, MATS, rows_y)),
            dma((2, 2, planes)),
            dma((2, MATS, planes)),
            dma((2, MATS + 1, rows_y, planes)),
            dma((2, MATS, rows_y, planes)),
            dma((2, back + 1)),
            dma((2, back + 1)),
            dma((2, back + 1)),
            dma((2, heads)),
            dma((2, 2)),
        ],
        compiler_params=pltpu.CompilerParams(
            collective_id=0, has_side_effects=True, vmem_limit_bytes=48 * 1024 * 1024
        ),
    )(
        held(qkv), held(token_rate.reshape(1, tokens)), head_rate, held(fast_state[:, 0])
    )
    return combined, new_state[:, None]


def solution(mesh):
    count, heads = mesh.shape["seq"], mesh.shape["head"]
    plane = CORES
    while plane * plane < count:
        plane *= 2
    planes = count // plane

    def whole(qkv, token_rate, head_rate, fast_state):
        plane_tokens = token_rate.shape[0] // planes
        back = min(-(-(WINDOW - 1) // plane_tokens), planes - 1)
        return jax.shard_map(
            functools.partial(shards, (heads, planes, plane, back)),
            mesh=mesh,
            in_specs=(
                P(None, ("seq", "head"), None),
                P("seq", "head"),
                P("head"),
                P(None, "head", "seq", None),
            ),
            out_specs=(P(("seq", "head"), None), P(None, "head", "seq", None)),
            check_vma=False,
        )(qkv, token_rate, head_rate, fast_state)

    return whole
```
